256 devices in a mesh: slab: 32 (over x, z), hodlr: 8 (over y, core).
Axes of the slice: x: 4, y: 4, z: 8, core: 2. Of those that a mesh axis runs over, the one named last changes fastest.
Arguments:
- sources: bfloat16 [32, 32, 16384], P('slab', None, 'hodlr'), may hold values from -2 to 2
- leaves: bfloat16 [32, 16, 1024, 1024], P('slab', 'hodlr'), may hold values from -1 to 2
- v_rows: bfloat16 [32, 4, 64, 16384], P('slab', None, None, 'hodlr'), may hold values from -0.0625 to 0.0625
- u_rows: bfloat16 [32, 4, 64, 16384], P('slab', None, None, 'hodlr'), may hold values from -0.1875 to 0.1875
Outputs:
- fronts: bfloat16 [32, 32, 16384], P('slab', None, 'hodlr')
The draws below stay inside these ranges and needn't reach their ends.
All inputs are finite; a program needn't handle non-finite values.
Results may differ from the reference program's by a relative error of at most 0.025.
Values may be sent and summed in bfloat16 or wider, within the bound.
A program may use at most 64 MiB of HBM per device.

```python
import math
import jax
import jax.numpy as jnp
from jax import lax

LEAF = 1024
BLOCK_RANK = 64
LEVELS = 4
SHOTS = 32
SLABS = 32
INTERFACE_SIZE = 16384
NLEAF = 16


def draw_leaves(key, part):
    shape = (SLABS, NLEAF, LEAF, LEAF)
    spread = jax.random.truncated_normal(key, -4.0, 4.0, shape, jnp.float32)
    unit = jnp.eye(LEAF, dtype=jnp.float32)
    return (0.85 * unit + 0.3 * spread / math.sqrt(LEAF)).astype(jnp.bfloat16)


def shard_levels(key, dims, cuts, smallest, largest):
    loudness = 1.0
    for dim, shards_of in cuts:
        steps = jax.random.uniform(jax.random.fold_in(jax.random.fold_in(key, 6), dim), (shards_of,), jnp.float32, smallest / len(cuts), largest / len(cuts))
        loudness = loudness * jnp.repeat(jnp.exp(steps), dims[dim] // shards_of).reshape((-1,) + (1,) * (len(dims) - 1 - dim))
    return loudness


def normal_values(own_key, dims, scale, most, split=(), held_as=jnp.bfloat16):
    result = jax.random.normal(own_key, dims, jnp.float32) * scale
    if len(split) > 0:
        result = shard_levels(own_key, dims, split, -0.22, 0.18) * result
    return jnp.clip(result, min=-most, max=most).astype(held_as)


def setup_inputs(seed: int = 0) -> dict:
    arg_keys = jax.random.split(jax.random.key(seed), 5)
    return {
        "sources": normal_values(arg_keys[0], (SLABS, SHOTS, INTERFACE_SIZE), 0.3, 2.0, ((0, 32), (2, 8))),
        "leaves": draw_leaves(jax.random.fold_in(arg_keys[4], 71), 0),
        "v_rows": normal_values(arg_keys[2], (SLABS, LEVELS, BLOCK_RANK, INTERFACE_SIZE), (INTERFACE_SIZE // 2) ** -0.5, 0.0625, ((0, 32), (3, 8))),
        "u_rows": normal_values(arg_keys[3], (SLABS, LEVELS, BLOCK_RANK, INTERFACE_SIZE), (16 * BLOCK_RANK) ** -0.5, 0.1875, ((0, 32), (3, 8))),
    }


def apply_slab(w, leaf, right_factor_transposed, left_factor_transposed):
    shot_batch = w.shape[0]
    wide_rows = w.astype(jnp.float32)
    sweep_output = jnp.einsum("sbj,bjo->sbo", wide_rows.reshape(shot_batch, NLEAF, LEAF), leaf.astype(jnp.float32), precision=lax.Precision.HIGHEST).reshape(shot_batch, INTERFACE_SIZE)
    for tree_level in range(1, LEVELS + 1):
        block_list = 2 ** tree_level
        block_size = INTERFACE_SIZE // block_list
        projection_rows = jnp.einsum("kqc,vqc->kqv", wide_rows.reshape(shot_batch, block_list, block_size), right_factor_transposed[tree_level - 1].astype(jnp.float32).reshape(BLOCK_RANK, block_list, block_size), precision=lax.Precision.HIGHEST)
        projection_rows = lax.optimization_barrier(projection_rows.astype(jnp.bfloat16)).astype(jnp.float32)
        swapped_halves = projection_rows.reshape(shot_batch, block_list // 2, 2, BLOCK_RANK)[:, :, ::-1].reshape(shot_batch, block_list, BLOCK_RANK)
        sweep_output = sweep_output + jnp.einsum("cwp,pwi->cwi", swapped_halves, left_factor_transposed[tree_level - 1].astype(jnp.float32).reshape(BLOCK_RANK, block_list, block_size), precision=lax.Precision.HIGHEST).reshape(shot_batch, INTERFACE_SIZE)
    return sweep_output.astype(jnp.bfloat16)


def reference(sources, leaves, v_rows, u_rows):
    def advance(front, inputs):
        source, leaf, right_factor_transposed, left_factor_transposed = inputs
        w = (source.astype(jnp.float32) + front.astype(jnp.float32)).astype(jnp.bfloat16)
        swept = apply_slab(w, leaf, right_factor_transposed, left_factor_transposed)
        return swept, swept

    start = jnp.zeros((SHOTS, INTERFACE_SIZE), jnp.bfloat16)
    _, fronts = lax.scan(advance, start, (sources, leaves, v_rows, u_rows))
    return fronts
```

```python
import functools

import jax
import jax.numpy as jnp
from jax import lax
from jax.experimental import pallas as pl
from jax.experimental.pallas import tpu as pltpu
from jax.sharding import PartitionSpec as P

MESH = pl.DeviceIdType.MESH
GROUPS = 4
WHOLE_SLABS = 5
PEERS = 8


def flipped(member, j):
    bits = (lax.rem(member, 2), lax.rem(lax.div(member, 2), 2), lax.div(member, 4))
    total = 0
    for i, bit in enumerate(bits):
        total = total + (1 << i) * ((1 - bit) if (j >> i) & 1 else bit)
    return total


def kernel(
    slabs, whole, src, leaf, v, u, out,
    u_prev, w_buf, l_in, p_in, p_self, l_send, l_wide, p_send, back, back_in,
    u_ss, u_rs, l_ss, l_rs, p_ss, p_rs, q_ss, q_rs, b_ss, b_rs,
):
    k = lax.axis_index("slab")
    m = lax.axis_index("hodlr")
    groups, rows, width = src.shape
    nleaf, size = leaf.shape[0], leaf.shape[1]

    first, last = k == 0, k == slabs - 1
    whole_send = k + 1 < whole
    split_send = jnp.logical_and(k + 1 >= whole, k < slabs - 1)
    whole_recv = jnp.logical_and(k >= 1, k < whole)
    split_recv = k >= whole
    own = jnp.logical_or(whole_send, last)

    def remote(source, target, send, recv, slab, member):
        return pltpu.make_async_remote_copy(
            src_ref=source, dst_ref=target, send_sem=send, recv_sem=recv,
            device_id=(slab, member), device_id_type=MESH,
        )

    def u_copy():
        return remote(u, u_prev, u_ss, u_rs, k + 1, m)

    def l_copy(g):
        return remote(l_send.at[g], l_in.at[g], l_ss.at[g], l_rs.at[g], k + 1, m)

    def back_copy(g):
        return remote(back.at[g], back_in.at[g], b_ss.at[g], b_rs.at[g], k - 1, m)

    def tile_of(j):
        return 1 if j == 1 else 0

    def p_copy(g, j):
        if j == 0:
            return remote(
                p_send.at[g, pl.ds(2, 2)], p_in.at[g, pl.ds(0, 2)], p_ss.at[g, 0], p_rs.at[g, 0], k + 1, m
            )
        return remote(
            p_send.at[g, tile_of(j)], p_in.at[g, j + 1], p_ss.at[g, j], p_rs.at[g, j], k + 1, flipped(m, j)
        )

    def q_copy(g, j):
        return remote(
            p_send.at[g, tile_of(j)], p_self.at[g, j], q_ss.at[g, j], q_rs.at[g, j], k, flipped(m, j)
        )

    barrier = pltpu.get_barrier_semaphore()

    def greet(slab, member):
        pl.semaphore_signal(barrier, inc=1, device_id=(slab, member), device_id_type=MESH)

    for j in range(1, PEERS):
        greet(k, flipped(m, j))

    @pl.when(k > 0)
    def _():
        for j in range(PEERS):
            greet(k - 1, flipped(m, j))

    @pl.when(k < slabs - 1)
    def _():
        for j in range(PEERS):
            greet(k + 1, flipped(m, j))

    edge = jnp.logical_or(first, last)

    @pl.when(edge)
    def _():
        pl.semaphore_wait(barrier, 2 * PEERS - 1)

    @pl.when(jnp.logical_not(edge))
    def _():
        pl.semaphore_wait(barrier, 3 * PEERS - 1)

    @pl.when(split_send)
    def _():
        u_copy().start()

    low = lax.broadcasted_iota(jnp.int32, (rows, 128), 1) < 64

    def low_rank(read, four_left, four_right, factors):
        one = read(4) + read(5) + read(6) + read(7)
        two = read(2) + read(3)
        three = read(1)
        top = jnp.where(low, one, two)
        left = jnp.concatenate([top, jnp.where(low, three, four_left)], axis=1).astype(jnp.bfloat16)
        right = jnp.concatenate([top, jnp.where(low, three, four_right)], axis=1).astype(jnp.bfloat16)
        return (
            jnp.dot(left, factors[:, :size], preferred_element_type=jnp.float32),
            jnp.dot(right, factors[:, size:], preferred_element_type=jnp.float32),
        )

    @pl.when(split_recv)
    def _():
        u_copy().wait_recv()

    @pl.loop(0, groups)
    def _(g):
        @pl.when(first)
        def _():
            w_buf[...] = src[g]

        @pl.when(whole_recv)
        def _():
            l_copy(g).wait_recv()
            w_buf[...] = (src[g].astype(jnp.float32) + l_in[g].astype(jnp.float32)).astype(jnp.bfloat16)

        @pl.when(split_recv)
        def _():
            for j in range(PEERS):
                p_copy(g, j).wait_recv()
            parts = low_rank(
                lambda j: p_in[g, j + 1].astype(jnp.float32),
                p_in[g, 0].astype(jnp.float32), p_in[g, 1].astype(jnp.float32), u_prev,
            )
            l_copy(g).wait_recv()
            for i, part in enumerate(parts):
                cols = slice(i * size, (i + 1) * size)
                front = (l_in[g, :, cols].astype(jnp.float32) + part).astype(jnp.bfloat16)
                back[g, :, cols] = front
                w_buf[:, cols] = (
                    src[g, :, cols].astype(jnp.float32) + front.astype(jnp.float32)
                ).astype(jnp.bfloat16)

        halves = [
            lax.dot_general(
                w_buf[:, i * size : (i + 1) * size], v[:, i * size : (i + 1) * size],
                (((1,), (1,)), ((), ())), preferred_element_type=jnp.float32,
            )
            for i in range(2)
        ]
        total = halves[0] + halves[1]
        p_send[g, 0] = total[:, :128].astype(jnp.bfloat16)
        p_send[g, 1] = total[:, 128:].astype(jnp.bfloat16)
        p_send[g, 2] = halves[1][:, 128:].astype(jnp.bfloat16)
        p_send[g, 3] = halves[0][:, 128:].astype(jnp.bfloat16)

        @pl.when(split_send)
        def _():
            for j in (6, 7, 4, 5, 2, 3, 1, 0):
                p_copy(g, j).start()

        @pl.when(own)
        def _():
            for j in (6, 7, 4, 5, 2, 3, 1):
                q_copy(g, j).start()

        for i in range(nleaf):
            cols = slice(i * size, (i + 1) * size)
            part = jnp.dot(w_buf[:, cols], leaf[i], preferred_element_type=jnp.float32)
            l_wide[g, :, cols] = part
            l_send[g, :, cols] = part.astype(jnp.bfloat16)

        @pl.when(split_send)
        def _():
            l_copy(g).start()

        @pl.when(split_recv)
        def _():
            back_copy(g).start()

    @pl.when(own)
    def _():
        @pl.loop(0, groups)
        def _(g):
            for j in range(1, PEERS):
                q_copy(g, j).wait_recv()
            parts = low_rank(
                lambda j: p_self[g, j].astype(jnp.float32),
                p_send[g, 2].astype(jnp.float32), p_send[g, 3].astype(jnp.float32), u,
            )
            for i, part in enumerate(parts):
                cols = slice(i * size, (i + 1) * size)
                front = (l_wide[g, :, cols] + part).astype(jnp.bfloat16)
                out[g, :, cols] = front
                l_send[g, :, cols] = front

            @pl.when(whole_send)
            def _():
                l_copy(g).start()

        @pl.loop(0, groups)
        def _(g):
            for j in range(1, PEERS):
                q_copy(g, j).wait_send()

            @pl.when(whole_send)
            def _():
                l_copy(g).wait_send()

    @pl.when(split_send)
    def _():
        u_copy().wait_send()

        @pl.loop(0, groups)
        def _(g):
            l_copy(g).wait_send()
            for j in range(PEERS):
                p_copy(g, j).wait_send()
            back_copy(g).wait_recv()
            out[g] = back_in[g]

    @pl.when(split_recv)
    def _():
        @pl.loop(0, groups)
        def _(g):
            back_copy(g).wait_send()


def solution(mesh, groups=GROUPS, whole=WHOLE_SLABS):
    slabs = mesh.shape["slab"]

    def local(sources, leaves, v_rows, u_rows):
        shots, width = sources.shape[1:]
        levels, rank = v_rows.shape[1:3]
        rows = shots // groups
        bf16, wide = jnp.bfloat16, jnp.float32
        dma = pltpu.SemaphoreType.DMA
        vmem = pl.BlockSpec(memory_space=pltpu.VMEM)
        swept = pl.pallas_call(
            functools.partial(kernel, slabs, whole),
            out_shape=jax.ShapeDtypeStruct((groups, rows, width), bf16),
            in_specs=[vmem] * 4,
            out_specs=vmem,
            scratch_shapes=[
                pltpu.VMEM((levels * rank, width), bf16),
                pltpu.VMEM((rows, width), bf16),
                pltpu.VMEM((groups, rows, width), bf16),
                pltpu.VMEM((groups, 9, rows, 128), bf16),
                pltpu.VMEM((groups, PEERS, rows, 128), bf16),
                pltpu.VMEM((groups, rows, width), bf16),
                pltpu.VMEM((groups, rows, width), wide),
                pltpu.VMEM((groups, 4, rows, 128), bf16),
                pltpu.VMEM((groups, rows, width), bf16),
                pltpu.VMEM((groups, rows, width), bf16),
                dma, dma,
                dma((groups,)), dma((groups,)),
                dma((groups, PEERS)), dma((groups, PEERS)),
                dma((groups, PEERS)), dma((groups, PEERS)),
                dma((groups,)), dma((groups,)),
            ],
            compiler_params=pltpu.CompilerParams(collective_id=0, has_side_effects=True),
            name="sweep",
        )(
            sources[0].reshape(groups, rows, width),
            leaves[0],
            v_rows[0].reshape(levels * rank, width),
            u_rows[0].reshape(levels * rank, width),
        )
        return swept.reshape(1, shots, width)

    return jax.shard_map(
        local,
        mesh=mesh,
        in_specs=(
            P("slab", None, "hodlr"),
            P("slab", "hodlr", None, None),
            P("slab", None, None, "hodlr"),
            P("slab", None, None, "hodlr"),
        ),
        out_specs=P("slab", None, "hodlr"),
        check_vma=False,
    )
```

```python
import functools

import jax
import jax.numpy as jnp
from jax import lax
from jax.experimental import pallas as pl
from jax.experimental.pallas import tpu as pltpu
from jax.sharding import PartitionSpec as P

MESH = pl.DeviceIdType.MESH
GROUPS = 4
WHOLE_SLABS = 4
PEERS = 8


def flipped(member, j):
    bits = (lax.rem(member, 2), lax.rem(lax.div(member, 2), 2), lax.div(member, 4))
    total = 0
    for i, bit in enumerate(bits):
        total = total + (1 << i) * ((1 - bit) if (j >> i) & 1 else bit)
    return total


def kernel(
    slabs, whole, src_hbm, leaf_hbm, v_hbm, u_hbm, out,
    src, leaf, v, u, load_sem, u_prev, w_buf, l_in, p_in, p_self, l_send, l_wide, p_send, back, back_in,
    u_ss, u_rs, l_ss, l_rs, p_ss, p_rs, q_ss, q_rs, b_ss, b_rs,
):
    k = lax.axis_index("slab")
    m = lax.axis_index("hodlr")
    groups, rows, width = src.shape
    nleaf, size = leaf.shape[0], leaf.shape[1]
    cross = u_prev.shape[0]
    bf16, wide = jnp.bfloat16, jnp.float32

    first, last = k == 0, k == slabs - 1
    whole_send = k + 1 < whole
    split_send = jnp.logical_and(k + 1 >= whole, k < slabs - 1)
    whole_recv = jnp.logical_and(k >= 1, k < whole)
    split_recv = k >= whole
    own = jnp.logical_or(whole_send, last)
    halves = [slice(i * size, (i + 1) * size) for i in range(nleaf)]

    def remote(source, target, send, recv, slab, member):
        return pltpu.make_async_remote_copy(
            src_ref=source, dst_ref=target, send_sem=send, recv_sem=recv,
            device_id=(slab, member), device_id_type=MESH,
        )

    def u_copy():
        return remote(u_hbm.at[pl.ds(0, cross)], u_prev, u_ss, u_rs, k + 1, m)

    def l_copy(g, i):
        return remote(l_send.at[g, i], l_in.at[g, i], l_ss.at[g, i], l_rs.at[g, i], k + 1, m)

    def back_copy(g):
        return remote(back.at[g], back_in.at[g], b_ss.at[g], b_rs.at[g], k - 1, m)

    def tile_of(j):
        return 1 if j == 1 else 0

    def p_copy(g, j):
        return remote(
            p_send.at[g, tile_of(j)], p_in.at[g, j], p_ss.at[g, j], p_rs.at[g, j], k + 1, flipped(m, j)
        )

    def q_copy(g, j):
        return remote(
            p_send.at[g, tile_of(j)], p_self.at[g, j], q_ss.at[g, j], q_rs.at[g, j], k, flipped(m, j)
        )

    loads = [
        pltpu.make_async_copy(source, target, load_sem.at[i])
        for i, (source, target) in enumerate(((src_hbm, src), (v_hbm, v), (leaf_hbm, leaf), (u_hbm, u)))
    ]
    for load in loads:
        load.start()

    barrier = pltpu.get_barrier_semaphore()

    def greet(slab, member):
        pl.semaphore_signal(barrier, inc=1, device_id=(slab, member), device_id_type=MESH)

    for j in range(1, PEERS):
        greet(k, flipped(m, j))

    @pl.when(k > 0)
    def _():
        for j in range(PEERS):
            greet(k - 1, flipped(m, j))

    @pl.when(k < slabs - 1)
    def _():
        for j in range(PEERS):
            greet(k + 1, flipped(m, j))

    edge = jnp.logical_or(first, last)

    @pl.when(edge)
    def _():
        pl.semaphore_wait(barrier, 2 * PEERS - 1)

    @pl.when(jnp.logical_not(edge))
    def _():
        pl.semaphore_wait(barrier, 3 * PEERS - 1)

    @pl.when(split_send)
    def _():
        u_copy().start()

    low = lax.broadcasted_iota(jnp.int32, (rows, 128), 1) < 64

    def low_rank(read, factors):
        one = read(4) + read(5) + read(6) + read(7)
        two = read(2) + read(3)
        top = jnp.where(low, one, two)
        both = jnp.concatenate([top, read(1)], axis=1).astype(bf16)[:, :cross]
        return [jnp.dot(both, factors[:cross, cols], preferred_element_type=wide) for cols in halves]

    for load in loads[:2]:
        load.wait()

    @pl.when(jnp.logical_not(first))
    def _():
        for load in loads[2:]:
            load.wait()

    @pl.when(split_recv)
    def _():
        u_copy().wait_recv()

    @pl.loop(0, groups)
    def _(g):
        @pl.when(first)
        def _():
            for i, cols in enumerate(halves):
                w_buf[g, i] = src[g, :, cols]

        @pl.when(whole_recv)
        def _():
            for i, cols in enumerate(halves):
                l_copy(g, i).wait_recv()
                w_buf[g, i] = (src[g, :, cols].astype(wide) + l_in[g, i].astype(wide)).astype(bf16)

        @pl.when(split_recv)
        def _():
            for j in range(1, PEERS):
                p_copy(g, j).wait_recv()
            parts = low_rank(lambda j: p_in[g, j].astype(wide), u_prev)
            for i, cols in enumerate(halves):
                l_copy(g, i).wait_recv()
                front = (l_in[g, i].astype(wide) + parts[i]).astype(bf16)
                back[g, i] = front
                w_buf[g, i] = (src[g, :, cols].astype(wide) + front.astype(wide)).astype(bf16)

        inner = [
            lax.dot_general(w_buf[g, i], v[:, cols], (((1,), (1,)), ((), ())), preferred_element_type=wide)
            for i, cols in enumerate(halves)
        ]
        total = inner[0] + inner[1]
        p_send[g, 0] = total[:, :128].astype(bf16)
        p_send[g, 1] = total[:, 128:].astype(bf16)
        for i in range(nleaf):
            p_send[g, 2 + i] = jnp.where(low, 0.0, inner[1 - i][:, 128:]).astype(bf16)

        @pl.when(split_send)
        def _():
            for j in (4, 6, 5, 7, 2, 3, 1):
                p_copy(g, j).start()

        @pl.when(own)
        def _():
            for j in (4, 6, 5, 7, 2, 3, 1):
                q_copy(g, j).start()

        @pl.when(split_send)
        def _():
            for i, cols in enumerate(halves):
                part = jnp.dot(w_buf[g, i], leaf[i], preferred_element_type=wide)
                part += jnp.dot(p_send[g, 2 + i], u[cross - 64 :, cols], preferred_element_type=wide)
                l_send[g, i] = part.astype(bf16)
                l_copy(g, i).start()

        @pl.when(split_recv)
        def _():
            back_copy(g).start()

    @pl.when(first)
    def _():
        for load in loads[2:]:
            load.wait()

    def stacked(array):
        return array.astype(wide).reshape(groups * rows, array.shape[-1]).astype(bf16)

    @pl.when(own)
    def _():
        for i, cols in enumerate(halves):
            part = jnp.dot(stacked(w_buf[:, i]), leaf[i], preferred_element_type=wide)
            part += jnp.dot(stacked(p_send[:, 2 + i]), u[cross - 64 :, cols], preferred_element_type=wide)
            l_wide[:, i] = part.reshape(groups, rows, size)

        @pl.loop(0, groups)
        def _(g):
            for j in range(1, PEERS):
                q_copy(g, j).wait_recv()
            parts = low_rank(lambda j: p_self[g, j].astype(wide), u)
            for i, cols in enumerate(halves):
                front = (l_wide[g, i] + parts[i]).astype(bf16)
                out[g, :, cols] = front
                l_send[g, i] = front

                @pl.when(whole_send)
                def _(i=i):
                    l_copy(g, i).start()

        @pl.loop(0, groups)
        def _(g):
            for j in range(1, PEERS):
                q_copy(g, j).wait_send()

            @pl.when(whole_send)
            def _():
                for i in range(nleaf):
                    l_copy(g, i).wait_send()

    @pl.when(split_send)
    def _():
        u_copy().wait_send()

        @pl.loop(0, groups)
        def _(g):
            for i in range(nleaf):
                l_copy(g, i).wait_send()
            for j in range(1, PEERS):
                p_copy(g, j).wait_send()
            back_copy(g).wait_recv()
            for i, cols in enumerate(halves):
                out[g, :, cols] = back_in[g, i]

    @pl.when(split_recv)
    def _():
        @pl.loop(0, groups)
        def _(g):
            back_copy(g).wait_send()


def solution(mesh, groups=GROUPS, whole=WHOLE_SLABS):
    slabs = mesh.shape["slab"]

    def local(sources, leaves, v_rows, u_rows):
        shots, width = sources.shape[1:]
        nleaf, size = leaves.shape[1:3]
        levels, rank = v_rows.shape[1:3]
        rows = shots // groups
        bf16, wide = jnp.bfloat16, jnp.float32
        dma = pltpu.SemaphoreType.DMA
        vmem = pl.BlockSpec(memory_space=pltpu.VMEM)

        def split(dtype):
            return pltpu.VMEM((groups, nleaf, rows, size), dtype)

        swept = pl.pallas_call(
            functools.partial(kernel, slabs, whole),
            out_shape=jax.ShapeDtypeStruct((groups, rows, width), bf16),
            in_specs=[pl.BlockSpec(memory_space=pl.ANY)] * 4,
            out_specs=vmem,
            scratch_shapes=[
                pltpu.VMEM((groups, rows, width), bf16),
                pltpu.VMEM((nleaf, size, size), bf16),
                pltpu.VMEM((levels * rank, width), bf16),
                pltpu.VMEM((levels * rank, width), bf16),
                dma((4,)),
                pltpu.VMEM(((levels - 1) * rank, width), bf16),
                split(bf16),
                split(bf16),
                pltpu.VMEM((groups, PEERS, rows, 128), bf16),
                pltpu.VMEM((groups, PEERS, rows, 128), bf16),
                split(bf16),
                split(wide),
                pltpu.VMEM((groups, 2 + nleaf, rows, 128), bf16),
                split(bf16),
                split(bf16),
                dma, dma,
                dma((groups, nleaf)), dma((groups, nleaf)),
                dma((groups, PEERS)), dma((groups, PEERS)),
                dma((groups, PEERS)), dma((groups, PEERS)),
                dma((groups,)), dma((groups,)),
            ],
            compiler_params=pltpu.CompilerParams(collective_id=0, has_side_effects=True),
            name="sweep",
        )(
            sources[0].reshape(groups, rows, width),
            leaves[0],
            v_rows[0].reshape(levels * rank, width),
            u_rows[0].reshape(levels * rank, width),
        )
        return swept.reshape(1, shots, width)

    return jax.shard_map(
        local,
        mesh=mesh,
        in_specs=(
            P("slab", None, "hodlr"),
            P("slab", "hodlr", None, None),
            P("slab", None, None, "hodlr"),
            P("slab", None, None, "hodlr"),
        ),
        out_specs=P("slab", None, "hodlr"),
        check_vma=False,
    )
```

```python
import functools

import jax
import jax.numpy as jnp
from jax import lax
from jax.experimental import pallas as pl
from jax.experimental.pallas import tpu as pltpu
from jax.sharding import PartitionSpec as P

MESH = pl.DeviceIdType.MESH
GROUPS = 4
WHOLE_SLABS = 4
PEERS = 8
ORDER = (4, 6, 5, 7, 2, 3, 1)


def flipped(member, j):
    bits = (lax.rem(member, 2), lax.rem(lax.div(member, 2), 2), lax.div(member, 4))
    total = 0
    for i, bit in enumerate(bits):
        total = total + (1 << i) * ((1 - bit) if (j >> i) & 1 else bit)
    return total


def kernel(
    slabs, whole, src_hbm, leaf_hbm, v_hbm, u_hbm, out,
    src, leaf, v, u, load_sem, u_prev, w_buf, l_in, p_in, p_self, l_send, l_wide, p_send, back, back_in,
    u_ss, u_rs, l_ss, l_rs, p_ss, p_rs, q_ss, q_rs, b_ss, b_rs,
):
    k = lax.axis_index("slab")
    m = lax.axis_index("hodlr")
    groups, rows, width = src.shape
    nleaf, size = leaf.shape[0], leaf.shape[1]
    cross = u_prev.shape[0]
    bf16, wide = jnp.bfloat16, jnp.float32

    first, last = k == 0, k == slabs - 1
    whole_send = k + 1 < whole
    split_send = jnp.logical_and(k + 1 >= whole, k < slabs - 1)
    whole_recv = jnp.logical_and(k >= 1, k < whole)
    split_recv = k >= whole
    own = jnp.logical_or(whole_send, last)
    halves = [slice(i * size, (i + 1) * size) for i in range(nleaf)]

    def remote(source, target, send, recv, slab, member):
        return pltpu.make_async_remote_copy(
            src_ref=source, dst_ref=target, send_sem=send, recv_sem=recv,
            device_id=(slab, member), device_id_type=MESH,
        )

    def u_copy():
        return remote(u_hbm.at[pl.ds(0, cross)], u_prev, u_ss, u_rs, k + 1, m)

    def l_copy(g, i):
        return remote(l_send.at[g, i], l_in.at[g, i], l_ss.at[g, i], l_rs.at[g, i], k + 1, m)

    def back_copy(g):
        return remote(back.at[g], back_in.at[g], b_ss.at[g], b_rs.at[g], k - 1, m)

    def tile_of(j):
        return 1 if j == 1 else 0

    def p_copy(g, j):
        return remote(
            p_send.at[g, tile_of(j)], p_in.at[g, j], p_ss.at[g, j], p_rs.at[g, j], k + 1, flipped(m, j)
        )

    def q_copy(g, j):
        return remote(
            p_send.at[g, tile_of(j)], p_self.at[g, j], q_ss.at[g, j], q_rs.at[g, j], k, flipped(m, j)
        )

    loads = [
        pltpu.make_async_copy(source, target, load_sem.at[i])
        for i, (source, target) in enumerate(((src_hbm, src), (v_hbm, v), (leaf_hbm, leaf), (u_hbm, u)))
    ]
    for load in loads:
        load.start()

    barrier = pltpu.get_barrier_semaphore()

    def greet(slab, member):
        pl.semaphore_signal(barrier, inc=1, device_id=(slab, member), device_id_type=MESH)

    @pl.when(own)
    def _():
        for j in range(1, PEERS):
            greet(k, flipped(m, j))

    @pl.when(whole_recv)
    def _():
        greet(k - 1, m)

    @pl.when(whole_send)
    def _():
        greet(k + 1, m)

    @pl.when(split_recv)
    def _():
        for j in range(PEERS):
            greet(k - 1, flipped(m, j))

    @pl.when(split_send)
    def _():
        for j in range(PEERS):
            greet(k + 1, flipped(m, j))

    met = (
        jnp.where(own, PEERS - 1, 0)
        + jnp.where(whole_recv, 1, 0) + jnp.where(whole_send, 1, 0)
        + jnp.where(split_recv, PEERS, 0) + jnp.where(split_send, PEERS, 0)
    )
    pl.semaphore_wait(barrier, met)

    @pl.when(split_send)
    def _():
        u_copy().start()

    low = lax.broadcasted_iota(jnp.int32, (rows, 128), 1) < 64

    def low_rank(read, factors):
        one = read(4) + read(5) + read(6) + read(7)
        two = read(2) + read(3)
        top = jnp.where(low, one, two)
        both = jnp.concatenate([top, read(1)], axis=1).astype(bf16)[:, :cross]
        return [jnp.dot(both, factors[:cross, cols], preferred_element_type=wide) for cols in halves]

    for load in loads[:2]:
        load.wait()

    @pl.when(jnp.logical_not(first))
    def _():
        for load in loads[2:]:
            load.wait()

    @pl.when(split_recv)
    def _():
        u_copy().wait_recv()

    def whole_in(g):
        pieces = []
        for i, cols in enumerate(halves):
            l_copy(g, i).wait_recv()
            pieces.append((src[g, :, cols].astype(wide) + l_in[g, i].astype(wide)).astype(bf16))
        return pieces

    def split_in(g):
        for j in range(1, PEERS):
            p_copy(g, j).wait_recv()
        for i in range(nleaf):
            l_copy(g, i).wait_recv()
        parts = low_rank(lambda j: p_in[g, j].astype(wide), u_prev)
        pieces = []
        for i, cols in enumerate(halves):
            front = (l_in[g, i].astype(wide) + parts[i]).astype(bf16)
            back[g, i] = front
            pieces.append((src[g, :, cols].astype(wide) + front.astype(wide)).astype(bf16))
        return pieces

    def project(g, w):
        inner = [
            lax.dot_general(w[i], v[:, cols], (((1,), (1,)), ((), ())), preferred_element_type=wide)
            for i, cols in enumerate(halves)
        ]
        total = inner[0] + inner[1]
        p_send[g, 0] = total[:, :128].astype(bf16)
        p_send[g, 1] = total[:, 128:].astype(bf16)
        return [jnp.where(low, 0.0, inner[1 - i][:, 128:]).astype(bf16) for i in range(nleaf)]

    def split_out(g, w):
        four = project(g, w)
        for j in ORDER:
            p_copy(g, j).start()
        for i, cols in enumerate(halves):
            part = jnp.dot(w[i], leaf[i], preferred_element_type=wide)
            part += jnp.dot(four[i], u[cross - 64 :, cols], preferred_element_type=wide)
            l_send[g, i] = part.astype(bf16)
            l_copy(g, i).start()

    @pl.when(jnp.logical_and(whole_recv, split_send))
    def _():
        @pl.loop(0, groups)
        def _(g):
            split_out(g, whole_in(g))

    @pl.when(jnp.logical_and(split_recv, split_send))
    def _():
        @pl.loop(0, groups)
        def _(g):
            split_out(g, split_in(g))
            back_copy(g).start()

    @pl.when(own)
    def _():
        @pl.loop(0, groups)
        def _(g):
            def keep(pieces):
                for i in range(nleaf):
                    w_buf[g, i] = pieces[i]

            @pl.when(first)
            def _():
                keep([src[g, :, cols] for cols in halves])

            @pl.when(whole_recv)
            def _():
                keep(whole_in(g))

            @pl.when(split_recv)
            def _():
                keep(split_in(g))

            for i, piece in enumerate(project(g, [w_buf[g, i] for i in range(nleaf)])):
                p_send[g, 2 + i] = piece
            for j in ORDER:
                q_copy(g, j).start()

            @pl.when(split_recv)
            def _():
                back_copy(g).start()

    @pl.when(first)
    def _():
        for load in loads[2:]:
            load.wait()

    def stacked(array):
        return array.astype(wide).reshape(groups * rows, array.shape[-1]).astype(bf16)

    @pl.when(own)
    def _():
        for i, cols in enumerate(halves):
            part = jnp.dot(stacked(w_buf[:, i]), leaf[i], preferred_element_type=wide)
            part += jnp.dot(stacked(p_send[:, 2 + i]), u[cross - 64 :, cols], preferred_element_type=wide)
            l_wide[:, i] = part.reshape(groups, rows, size)

        @pl.loop(0, groups)
        def _(g):
            for j in range(1, PEERS):
                q_copy(g, j).wait_recv()
            parts = low_rank(lambda j: p_self[g, j].astype(wide), u)
            for i, cols in enumerate(halves):
                front = (l_wide[g, i] + parts[i]).astype(bf16)
                out[g, :, cols] = front
                l_send[g, i] = front

                @pl.when(whole_send)
                def _(i=i):
                    l_copy(g, i).start()

        @pl.loop(0, groups)
        def _(g):
            for j in range(1, PEERS):
                q_copy(g, j).wait_send()

            @pl.when(whole_send)
            def _():
                for i in range(nleaf):
                    l_copy(g, i).wait_send()

    @pl.when(split_send)
    def _():
        u_copy().wait_send()

        @pl.loop(0, groups)
        def _(g):
            for i in range(nleaf):
                l_copy(g, i).wait_send()
            for j in range(1, PEERS):
                p_copy(g, j).wait_send()
            back_copy(g).wait_recv()
            for i, cols in enumerate(halves):
                out[g, :, cols] = back_in[g, i]

    @pl.when(split_recv)
    def _():
        @pl.loop(0, groups)
        def _(g):
            back_copy(g).wait_send()


def solution(mesh, groups=GROUPS, whole=WHOLE_SLABS):
    slabs = mesh.shape["slab"]

    def local(sources, leaves, v_rows, u_rows):
        shots, width = sources.shape[1:]
        nleaf, size = leaves.shape[1:3]
        levels, rank = v_rows.shape[1:3]
        rows = shots // groups
        bf16, wide = jnp.bfloat16, jnp.float32
        dma = pltpu.SemaphoreType.DMA
        vmem = pl.BlockSpec(memory_space=pltpu.VMEM)

        def split(dtype):
            return pltpu.VMEM((groups, nleaf, rows, size), dtype)

        swept = pl.pallas_call(
            functools.partial(kernel, slabs, whole),
            out_shape=jax.ShapeDtypeStruct((groups, rows, width), bf16),
            in_specs=[pl.BlockSpec(memory_space=pl.ANY)] * 4,
            out_specs=vmem,
            scratch_shapes=[
                pltpu.VMEM((groups, rows, width), bf16),
                pltpu.VMEM((nleaf, size, size), bf16),
                pltpu.VMEM((levels * rank, width), bf16),
                pltpu.VMEM((levels * rank, width), bf16),
                dma((4,)),
                pltpu.VMEM(((levels - 1) * rank, width), bf16),
                split(bf16),
                split(bf16),
                pltpu.VMEM((groups, PEERS, rows, 128), bf16),
                pltpu.VMEM((groups, PEERS, rows, 128), bf16),
                split(bf16),
                split(wide),
                pltpu.VMEM((groups, 2 + nleaf, rows, 128), bf16),
                split(bf16),
                split(bf16),
                dma, dma,
                dma((groups, nleaf)), dma((groups, nleaf)),
                dma((groups, PEERS)), dma((groups, PEERS)),
                dma((groups, PEERS)), dma((groups, PEERS)),
                dma((groups,)), dma((groups,)),
            ],
            compiler_params=pltpu.CompilerParams(collective_id=0, has_side_effects=True),
            name="sweep",
        )(
            sources[0].reshape(groups, rows, width),
            leaves[0],
            v_rows[0].reshape(levels * rank, width),
            u_rows[0].reshape(levels * rank, width),
        )
        return swept.reshape(1, shots, width)

    return jax.shard_map(
        local,
        mesh=mesh,
        in_specs=(
            P("slab", None, "hodlr"),
            P("slab", "hodlr", None, None),
            P("slab", None, None, "hodlr"),
            P("slab", None, None, "hodlr"),
        ),
        out_specs=P("slab", None, "hodlr"),
        check_vma=False,
    )
```

```python
import functools

import jax
import jax.numpy as jnp
from jax import lax
from jax.experimental import pallas as pl
from jax.experimental.pallas import tpu as pltpu
from jax.sharding import PartitionSpec as P

MESH = pl.DeviceIdType.MESH
GROUPS = 4
WHOLE_SLABS = 4
PEERS = 8
CHUNKS = 1
ORDER = (4, 6, 5, 7, 2, 3, 1)


def flipped(member, j):
    bits = (lax.rem(member, 2), lax.rem(lax.div(member, 2), 2), lax.div(member, 4))
    total = 0
    for i, bit in enumerate(bits):
        total = total + (1 << i) * ((1 - bit) if (j >> i) & 1 else bit)
    return total


def kernel(
    slabs, whole, src_hbm, leaf_hbm, v_hbm, u_hbm, out,
    src, leaf, v, u, src_sem, leaf_sem, v_sem, u_sem, u_prev, mixed, w_buf, l_in, p_in, p_self, l_send, l_wide, p_send, back, back_in,
    u_ss, u_rs, l_ss, l_rs, p_ss, p_rs, q_ss, q_rs, b_ss, b_rs,
):
    k = lax.axis_index("slab")
    m = lax.axis_index("hodlr")
    groups, rows, width = src.shape
    nleaf, strips, size, _ = leaf.shape
    cross = u_prev.shape[1]
    bf16, wide = jnp.bfloat16, jnp.float32

    first, last = k == 0, k == slabs - 1
    whole_send = k + 1 < whole
    split_send = jnp.logical_and(k + 1 >= whole, k < slabs - 1)
    whole_recv = jnp.logical_and(k >= 1, k < whole)
    split_recv = k >= whole
    own = jnp.logical_or(whole_send, last)
    chunks, part_width = l_in.shape[1], l_in.shape[3]
    per_leaf, lanes = chunks // nleaf, part_width // 128
    spans = [slice(c * part_width, (c + 1) * part_width) for c in range(chunks)]

    def remote(source, target, send, recv, slab, member):
        return pltpu.make_async_remote_copy(
            src_ref=source, dst_ref=target, send_sem=send, recv_sem=recv,
            device_id=(slab, member), device_id_type=MESH,
        )

    def u_copy():
        return remote(u.at[:, pl.ds(0, cross)], u_prev, u_ss, u_rs, k + 1, m)

    def l_copy(g, i):
        return remote(l_send.at[g, i], l_in.at[g, i], l_ss.at[g, i], l_rs.at[g, i], k + 1, m)

    def back_copy(g):
        return remote(back.at[g], back_in.at[g], b_ss.at[g], b_rs.at[g], k - 1, m)

    def tile_of(j):
        return 1 if j == 1 else 0

    def p_copy(g, j):
        return remote(
            p_send.at[g, tile_of(j)], p_in.at[g, j], p_ss.at[g, j], p_rs.at[g, j], k + 1, flipped(m, j)
        )

    def q_copy(g, j):
        return remote(
            p_send.at[g, tile_of(j)], p_self.at[g, j], q_ss.at[g, j], q_rs.at[g, j], k, flipped(m, j)
        )

    def strip(source, target, t, sem):
        return pltpu.make_async_copy(source.at[:, pl.ds(t * 128, 128)], target.at[t], sem)

    loads = [
        [pltpu.make_async_copy(src_hbm, src, src_sem)],
        [strip(v_hbm, v, t, v_sem.at[t]) for t in range(nleaf * strips)],
        [strip(leaf_hbm.at[i], leaf.at[i], t, leaf_sem.at[i, t]) for i in range(nleaf) for t in range(strips)],
        [strip(u_hbm, u, t, u_sem.at[t]) for t in range(nleaf * strips)],
    ]

    def arrived(parts):
        for part in parts:
            for load in part:
                load.wait()

    def begin(parts):
        for part in parts:
            for load in part:
                load.start()

    begin(loads[:2])

    @pl.when(jnp.logical_not(first))
    def _():
        begin((loads[3], loads[2]))

    def joined(ref, c, *rows_of):
        return jnp.concatenate([ref[(c * lanes + t, *rows_of)] for t in range(lanes)], axis=1)

    def side(pieces, i):
        return jnp.concatenate(pieces[i * per_leaf : (i + 1) * per_leaf], axis=1)

    barrier = pltpu.get_barrier_semaphore()

    def greet(slab, member):
        pl.semaphore_signal(barrier, inc=1, device_id=(slab, member), device_id_type=MESH)

    @pl.when(own)
    def _():
        for j in range(1, PEERS):
            greet(k, flipped(m, j))

    @pl.when(whole_recv)
    def _():
        greet(k - 1, m)

    @pl.when(whole_send)
    def _():
        greet(k + 1, m)

    @pl.when(split_recv)
    def _():
        for j in range(PEERS):
            greet(k - 1, flipped(m, j))

    @pl.when(split_send)
    def _():
        for j in range(PEERS):
            greet(k + 1, flipped(m, j))

    met = (
        jnp.where(own, PEERS - 1, 0)
        + jnp.where(whole_recv, 1, 0) + jnp.where(whole_send, 1, 0)
        + jnp.where(split_recv, PEERS, 0) + jnp.where(split_send, PEERS, 0)
    )
    pl.semaphore_wait(barrier, met)

    @pl.when(split_send)
    def _():
        arrived(loads[3:])
        u_copy().start()

    low = lax.broadcasted_iota(jnp.int32, (rows, 128), 1) < 64

    def shared(read):
        one = read(4) + read(5) + read(6) + read(7)
        two = read(2) + read(3)
        top = jnp.where(low, one, two)
        return jnp.concatenate([top, read(1)], axis=1).astype(bf16)[:, :cross]

    def low_rank(both, factors):
        return [
            jnp.dot(both, joined(factors, c, slice(0, cross)), preferred_element_type=wide) for c in range(chunks)
        ]

    arrived(loads[:2])

    @pl.when(first)
    def _():
        begin(loads[2:])

    @pl.when(jnp.logical_not(first))
    def _():
        arrived(loads[2:3])

    @pl.when(split_recv)
    def _():
        u_copy().wait_recv()

    def added_to_source(g, c, front):
        return (src[g, :, spans[c]].astype(wide) + front.astype(wide)).astype(bf16)

    def whole_in(g):
        pieces = []
        for c in range(chunks):
            l_copy(g, c).wait_recv()
            pieces.append(added_to_source(g, c, l_in[g, c]))
        return pieces

    def completed(g, parts):
        pieces = []
        for c in range(chunks):
            front = (l_in[g, c].astype(wide) + parts[c]).astype(bf16)
            back[g, c] = front
            pieces.append(added_to_source(g, c, front))
        return pieces

    def split_in(g):
        for j in range(1, PEERS):
            p_copy(g, j).wait_recv()
        for c in range(chunks):
            l_copy(g, c).wait_recv()
        return completed(g, low_rank(shared(lambda j: p_in[g, j].astype(wide)), u_prev))

    def one_inner(piece, c):
        return lax.dot_general(piece, joined(v, c), (((1,), (1,)), ((), ())), preferred_element_type=wide)

    def inner_of(pieces):
        inner = []
        for i in range(nleaf):
            terms = [one_inner(pieces[c], c) for c in range(i * per_leaf, (i + 1) * per_leaf)]
            inner.append(functools.reduce(jnp.add, terms))
        return inner

    def project(g, pieces):
        inner = inner_of(pieces)
        total = inner[0] + inner[1]
        p_send[g, 0] = total[:, :128].astype(bf16)
        p_send[g, 1] = total[:, 128:].astype(bf16)
        return [jnp.where(low, 0.0, inner[1 - i][:, 128:]).astype(bf16) for i in range(nleaf)]

    def block_part(piece, four, c):
        i, first_strip = c // per_leaf, (c % per_leaf) * lanes
        factor = jnp.concatenate([leaf[i, first_strip + t] for t in range(lanes)], axis=1)
        part = jnp.dot(piece, factor, preferred_element_type=wide)
        return part + jnp.dot(four, joined(u, c, slice(cross - 64, None)), preferred_element_type=wide)

    def send_parts(g, pieces, four):
        for i in range(nleaf):
            piece = side(pieces, i)
            for c in range(i * per_leaf, (i + 1) * per_leaf):
                l_send[g, c] = block_part(piece, four[i], c).astype(bf16)
                l_copy(g, c).start()

    def split_out(g, pieces):
        four = project(g, pieces)
        for j in ORDER:
            p_copy(g, j).start()
        send_parts(g, pieces, four)

    @pl.when(jnp.logical_and(whole_recv, split_send))
    def _():
        @pl.loop(0, groups)
        def _(g):
            split_out(g, whole_in(g))

    @pl.when(k == whole)
    def _():
        @pl.loop(0, groups)
        def _(g):
            split_out(g, split_in(g))
            back_copy(g).start()

    @pl.when(jnp.logical_and(k > whole, split_send))
    def _():
        inner = inner_of([joined(u_prev, c) for c in range(chunks)])
        total = (inner[0] + inner[1]).astype(bf16)
        mixed[0] = total[:, :128]
        mixed[1] = total[:, 128:]
        mixed[2] = inner[1][:, 128:].astype(bf16)
        mixed[3] = inner[0][:, 128:].astype(bf16)

        @pl.loop(0, groups)
        def _(g):
            terms = []
            for c in range(chunks):
                l_copy(g, c).wait_recv()
                terms.append(one_inner(added_to_source(g, c, l_in[g, c]), c))
            base = [functools.reduce(jnp.add, terms[i * per_leaf : (i + 1) * per_leaf]) for i in range(nleaf)]
            ready = base[0] + base[1]
            for j in range(1, PEERS):
                p_copy(g, j).wait_recv()
            both = shared(lambda j: p_in[g, j].astype(wide))
            added = jnp.dot(both, jnp.concatenate([mixed[t] for t in range(4)], axis=1), preferred_element_type=wide)
            p_send[g, 0] = (ready[:, :128] + added[:, :128]).astype(bf16)
            p_send[g, 1] = (ready[:, 128:] + added[:, 128:256]).astype(bf16)
            for j in ORDER:
                p_copy(g, j).start()
            pieces = completed(g, low_rank(both, u_prev))
            four = []
            for i in range(nleaf):
                value = base[1 - i][:, 128:] + added[:, 256 + 128 * i : 384 + 128 * i]
                four.append(jnp.where(low, 0.0, value).astype(bf16))
            send_parts(g, pieces, four)
            back_copy(g).start()

    @pl.when(own)
    def _():
        @pl.loop(0, groups)
        def _(g):
            def keep(pieces):
                for c in range(chunks):
                    w_buf[g, c] = pieces[c]

            @pl.when(first)
            def _():
                keep([src[g, :, span] for span in spans])

            @pl.when(whole_recv)
            def _():
                keep(whole_in(g))

            @pl.when(split_recv)
            def _():
                keep(split_in(g))

            for i, piece in enumerate(project(g, [w_buf[g, c] for c in range(chunks)])):
                p_send[g, 2 + i] = piece
            for j in ORDER:
                q_copy(g, j).start()

            @pl.when(split_recv)
            def _():
                back_copy(g).start()

    @pl.when(first)
    def _():
        arrived(loads[2:3])

    @pl.when(own)
    def _():
        arrived(loads[3:])

    def stacked(array):
        return array.astype(wide).reshape(groups * rows, array.shape[-1]).astype(bf16)

    @pl.when(own)
    def _():
        for i in range(nleaf):
            piece = jnp.concatenate(
                [stacked(w_buf[:, c]) for c in range(i * per_leaf, (i + 1) * per_leaf)], axis=1
            )
            four = stacked(p_send[:, 2 + i])
            for c in range(i * per_leaf, (i + 1) * per_leaf):
                l_wide[:, c] = block_part(piece, four, c).reshape(groups, rows, part_width)

        @pl.loop(0, groups)
        def _(g):
            for j in range(1, PEERS):
                q_copy(g, j).wait_recv()
            parts = low_rank(shared(lambda j: p_self[g, j].astype(wide)), u)
            for c, span in enumerate(spans):
                front = (l_wide[g, c] + parts[c]).astype(bf16)
                out[g, :, span] = front
                l_send[g, c] = front

                @pl.when(whole_send)
                def _(c=c):
                    l_copy(g, c).start()

        @pl.loop(0, groups)
        def _(g):
            for j in range(1, PEERS):
                q_copy(g, j).wait_send()

            @pl.when(whole_send)
            def _():
                for c in range(chunks):
                    l_copy(g, c).wait_send()

    @pl.when(split_send)
    def _():
        u_copy().wait_send()

        @pl.loop(0, groups)
        def _(g):
            for c in range(chunks):
                l_copy(g, c).wait_send()
            for j in range(1, PEERS):
                p_copy(g, j).wait_send()
            back_copy(g).wait_recv()
            for c, span in enumerate(spans):
                out[g, :, span] = back_in[g, c]

    @pl.when(split_recv)
    def _():
        @pl.loop(0, groups)
        def _(g):
            back_copy(g).wait_send()


def solution(mesh, groups=GROUPS, whole=WHOLE_SLABS):
    slabs = mesh.shape["slab"]

    def local(sources, leaves, v_rows, u_rows):
        shots, width = sources.shape[1:]
        nleaf, size = leaves.shape[1:3]
        levels, rank = v_rows.shape[1:3]
        rows = shots // groups
        bf16, wide = jnp.bfloat16, jnp.float32
        dma = pltpu.SemaphoreType.DMA
        vmem = pl.BlockSpec(memory_space=pltpu.VMEM)

        def split(dtype):
            return pltpu.VMEM((groups, CHUNKS * nleaf, rows, size // CHUNKS), dtype)

        swept = pl.pallas_call(
            functools.partial(kernel, slabs, whole),
            out_shape=jax.ShapeDtypeStruct((groups, rows, width), bf16),
            in_specs=[pl.BlockSpec(memory_space=pl.ANY)] * 4,
            out_specs=vmem,
            scratch_shapes=[
                pltpu.VMEM((groups, rows, width), bf16),
                pltpu.VMEM((nleaf, size // 128, size, 128), bf16),
                pltpu.VMEM((width // 128, levels * rank, 128), bf16),
                pltpu.VMEM((width // 128, levels * rank, 128), bf16),
                dma, dma((nleaf, size // 128)), dma((width // 128,)), dma((width // 128,)),
                pltpu.VMEM((width // 128, (levels - 1) * rank, 128), bf16),
                pltpu.VMEM((4, (levels - 1) * rank, 128), bf16),
                split(bf16),
                split(bf16),
                pltpu.VMEM((groups, PEERS, rows, 128), bf16),
                pltpu.VMEM((groups, PEERS, rows, 128), bf16),
                split(bf16),
                split(wide),
                pltpu.VMEM((groups, 2 + nleaf, rows, 128), bf16),
                split(bf16),
                split(bf16),
                dma, dma,
                dma((groups, CHUNKS * nleaf)), dma((groups, CHUNKS * nleaf)),
                dma((groups, PEERS)), dma((groups, PEERS)),
                dma((groups, PEERS)), dma((groups, PEERS)),
                dma((groups,)), dma((groups,)),
            ],
            compiler_params=pltpu.CompilerParams(collective_id=0, has_side_effects=True),
            name="sweep",
        )(
            sources[0].reshape(groups, rows, width),
            leaves[0],
            v_rows[0].reshape(levels * rank, width),
            u_rows[0].reshape(levels * rank, width),
        )
        return swept.reshape(1, shots, width)

    return jax.shard_map(
        local,
        mesh=mesh,
        in_specs=(
            P("slab", None, "hodlr"),
            P("slab", "hodlr", None, None),
            P("slab", None, None, "hodlr"),
            P("slab", None, None, "hodlr"),
        ),
        out_specs=P("slab", None, "hodlr"),
        check_vma=False,
    )
```

```python
import functools

import jax
import jax.numpy as jnp
from jax import lax
from jax.experimental import pallas as pl
from jax.experimental.pallas import tpu as pltpu
from jax.sharding import PartitionSpec as P

MESH = pl.DeviceIdType.MESH
GROUPS = 4
WHOLE_SLABS = 4
PEERS = 8
CHUNKS = 1
ORDER = (4, 6, 5, 7, 2, 3, 1)


def flipped(member, j):
    bits = (lax.rem(member, 2), lax.rem(lax.div(member, 2), 2), lax.div(member, 4))
    total = 0
    for i, bit in enumerate(bits):
        total = total + (1 << i) * ((1 - bit) if (j >> i) & 1 else bit)
    return total


def kernel(
    slabs, whole, src_hbm, leaf_hbm, v_hbm, u_hbm, out,
    src, leaf, v, u, src_sem, leaf_sem, v_sem, u_sem, u_prev, mixed, w_buf, l_in, p_in, p_self, l_send, l_wide, p_send, back, back_in,
    u_ss, u_rs, l_ss, l_rs, p_ss, p_rs, q_ss, q_rs, b_ss, b_rs,
):
    k = lax.axis_index("slab")
    m = lax.axis_index("hodlr")
    groups, rows, width = src.shape
    nleaf, strips, size, _ = leaf.shape
    cross = u_prev.shape[1]
    bf16, wide = jnp.bfloat16, jnp.float32

    first, last = k == 0, k == slabs - 1
    whole_send = k + 1 < whole
    split_send = jnp.logical_and(k + 1 >= whole, k < slabs - 1)
    whole_recv = jnp.logical_and(k >= 1, k < whole)
    split_recv = k >= whole
    own = jnp.logical_or(whole_send, last)
    chunks, part_width = l_in.shape[1], l_in.shape[3]
    per_leaf, lanes = chunks // nleaf, part_width // 128
    spans = [slice(c * part_width, (c + 1) * part_width) for c in range(chunks)]

    def remote(source, target, send, recv, slab, member):
        return pltpu.make_async_remote_copy(
            src_ref=source, dst_ref=target, send_sem=send, recv_sem=recv,
            device_id=(slab, member), device_id_type=MESH,
        )

    def u_copy():
        return remote(u.at[:, pl.ds(0, cross)], u_prev, u_ss, u_rs, k + 1, m)

    def l_copy(g, i):
        return remote(l_send.at[g, i], l_in.at[g, i], l_ss.at[g, i], l_rs.at[g, i], k + 1, m)

    def back_copy(g):
        return remote(back.at[g], back_in.at[g], b_ss.at[g], b_rs.at[g], k - 1, m)

    def tile_of(j):
        return 1 if j == 1 else 0

    def p_copy(g, j):
        return remote(
            p_send.at[g, tile_of(j)], p_in.at[g, j], p_ss.at[g, j], p_rs.at[g, j], k + 1, flipped(m, j)
        )

    def q_copy(g, j):
        return remote(
            p_send.at[g, tile_of(j)], p_self.at[g, j], q_ss.at[g, j], q_rs.at[g, j], k, flipped(m, j)
        )

    def strip(source, target, t, sem):
        return pltpu.make_async_copy(source.at[:, pl.ds(t * 128, 128)], target.at[t], sem)

    loads = [
        [pltpu.make_async_copy(src_hbm, src, src_sem)],
        [strip(v_hbm, v, t, v_sem.at[t]) for t in range(nleaf * strips)],
        [strip(leaf_hbm.at[i], leaf.at[i], t, leaf_sem.at[i, t]) for i in range(nleaf) for t in range(strips)],
        [strip(u_hbm, u, t, u_sem.at[t]) for t in range(nleaf * strips)],
    ]

    def arrived(parts):
        for part in parts:
            for load in part:
                load.wait()

    def begin(parts):
        for part in parts:
            for load in part:
                load.start()

    begin(loads[:2])

    @pl.when(jnp.logical_not(first))
    def _():
        begin((loads[3], loads[2]))

    def joined(ref, c, *rows_of):
        return jnp.concatenate([ref[(c * lanes + t, *rows_of)] for t in range(lanes)], axis=1)

    def side(pieces, i):
        return jnp.concatenate(pieces[i * per_leaf : (i + 1) * per_leaf], axis=1)

    barrier = pltpu.get_barrier_semaphore()

    def greet(slab, member):
        pl.semaphore_signal(barrier, inc=1, device_id=(slab, member), device_id_type=MESH)

    @pl.when(own)
    def _():
        for j in range(1, PEERS):
            greet(k, flipped(m, j))

    @pl.when(whole_recv)
    def _():
        greet(k - 1, m)

    @pl.when(whole_send)
    def _():
        greet(k + 1, m)

    @pl.when(split_recv)
    def _():
        for j in range(PEERS):
            greet(k - 1, flipped(m, j))

    @pl.when(split_send)
    def _():
        for j in range(PEERS):
            greet(k + 1, flipped(m, j))

    low = lax.broadcasted_iota(jnp.int32, (rows, 128), 1) < 64

    def shared(read):
        one = read(4) + read(5) + read(6) + read(7)
        two = read(2) + read(3)
        top = jnp.where(low, one, two)
        return jnp.concatenate([top, read(1)], axis=1).astype(bf16)[:, :cross]

    def low_rank(both, factors):
        return [
            jnp.dot(both, joined(factors, c, slice(0, cross)), preferred_element_type=wide) for c in range(chunks)
        ]


    def added_to_source(g, c, front):
        return (src[g, :, spans[c]].astype(wide) + front.astype(wide)).astype(bf16)

    def whole_in(g):
        pieces = []
        for c in range(chunks):
            l_copy(g, c).wait_recv()
            pieces.append(added_to_source(g, c, l_in[g, c]))
        return pieces

    def completed(g, parts):
        pieces = []
        for c in range(chunks):
            front = (l_in[g, c].astype(wide) + parts[c]).astype(bf16)
            back[g, c] = front
            pieces.append(added_to_source(g, c, front))
        return pieces

    def split_in(g):
        for j in range(1, PEERS):
            p_copy(g, j).wait_recv()
        for c in range(chunks):
            l_copy(g, c).wait_recv()
        return completed(g, low_rank(shared(lambda j: p_in[g, j].astype(wide)), u_prev))

    def one_inner(piece, c):
        return lax.dot_general(piece, joined(v, c), (((1,), (1,)), ((), ())), preferred_element_type=wide)

    def inner_of(pieces):
        inner = []
        for i in range(nleaf):
            terms = [one_inner(pieces[c], c) for c in range(i * per_leaf, (i + 1) * per_leaf)]
            inner.append(functools.reduce(jnp.add, terms))
        return inner

    def project(g, pieces):
        inner = inner_of(pieces)
        total = inner[0] + inner[1]
        p_send[g, 0] = total[:, :128].astype(bf16)
        p_send[g, 1] = total[:, 128:].astype(bf16)
        return [jnp.where(low, 0.0, inner[1 - i][:, 128:]).astype(bf16) for i in range(nleaf)]

    def block_part(piece, four, c):
        i, first_strip = c // per_leaf, (c % per_leaf) * lanes
        factor = jnp.concatenate([leaf[i, first_strip + t] for t in range(lanes)], axis=1)
        part = jnp.dot(piece, factor, preferred_element_type=wide)
        return part + jnp.dot(four, joined(u, c, slice(cross - 64, None)), preferred_element_type=wide)

    def send_parts(g, pieces, four):
        for i in range(nleaf):
            piece = side(pieces, i)
            for c in range(i * per_leaf, (i + 1) * per_leaf):
                l_send[g, c] = block_part(piece, four[i], c).astype(bf16)
                l_copy(g, c).start()

    def split_out(g, pieces):
        four = project(g, pieces)
        for j in ORDER:
            p_copy(g, j).start()
        send_parts(g, pieces, four)

    @pl.when(first)
    def _():
        arrived(loads[:2])
        begin(loads[2:])

    met = (
        jnp.where(own, PEERS - 1, 0)
        + jnp.where(whole_recv, 1, 0) + jnp.where(whole_send, 1, 0)
        + jnp.where(split_recv, PEERS, 0) + jnp.where(split_send, PEERS, 0)
    )
    pl.semaphore_wait(barrier, met)

    @pl.when(split_send)
    def _():
        arrived(loads[3:])
        u_copy().start()

    @pl.when(jnp.logical_not(first))
    def _():
        arrived(loads[:3])

    @pl.when(split_recv)
    def _():
        u_copy().wait_recv()

    @pl.when(jnp.logical_and(whole_recv, split_send))
    def _():
        @pl.loop(0, groups)
        def _(g):
            split_out(g, whole_in(g))

    @pl.when(k == whole)
    def _():
        @pl.loop(0, groups)
        def _(g):
            split_out(g, split_in(g))
            back_copy(g).start()

    def mixed_projection(g):
        terms = []
        for c in range(chunks):
            l_copy(g, c).wait_recv()
            terms.append(one_inner(added_to_source(g, c, l_in[g, c]), c))
        base = [functools.reduce(jnp.add, terms[i * per_leaf : (i + 1) * per_leaf]) for i in range(nleaf)]
        ready = base[0] + base[1]
        for j in range(1, PEERS):
            p_copy(g, j).wait_recv()
        both = shared(lambda j: p_in[g, j].astype(wide))
        added = jnp.dot(both, jnp.concatenate([mixed[t] for t in range(4)], axis=1), preferred_element_type=wide)
        p_send[g, 0] = (ready[:, :128] + added[:, :128]).astype(bf16)
        p_send[g, 1] = (ready[:, 128:] + added[:, 128:256]).astype(bf16)
        return base, added, both

    def mixed_four(base, added):
        four = []
        for i in range(nleaf):
            value = base[1 - i][:, 128:] + added[:, 256 + 128 * i : 384 + 128 * i]
            four.append(jnp.where(low, 0.0, value).astype(bf16))
        return four

    @pl.when(k > whole)
    def _():
        inner = inner_of([joined(u_prev, c) for c in range(chunks)])
        total = (inner[0] + inner[1]).astype(bf16)
        mixed[0] = total[:, :128]
        mixed[1] = total[:, 128:]
        mixed[2] = inner[1][:, 128:].astype(bf16)
        mixed[3] = inner[0][:, 128:].astype(bf16)

    @pl.when(jnp.logical_and(k > whole, split_send))
    def _():
        @pl.loop(0, groups)
        def _(g):
            base, added, both = mixed_projection(g)
            for j in ORDER:
                p_copy(g, j).start()
            pieces = completed(g, low_rank(both, u_prev))
            send_parts(g, pieces, mixed_four(base, added))
            back_copy(g).start()

    @pl.when(first)
    def _():
        @pl.loop(0, groups)
        def _(g):
            pieces = [src[g, :, span] for span in spans]
            for i, piece in enumerate(project(g, pieces)):
                p_send[g, 2 + i] = piece
            for j in ORDER:
                q_copy(g, j).start()
            for c in range(chunks):
                w_buf[g, c] = pieces[c]

    @pl.when(jnp.logical_and(whole_recv, whole_send))
    def _():
        @pl.loop(0, groups)
        def _(g):
            pieces = whole_in(g)
            for i, piece in enumerate(project(g, pieces)):
                p_send[g, 2 + i] = piece
            for j in ORDER:
                q_copy(g, j).start()
            for c in range(chunks):
                w_buf[g, c] = pieces[c]

    @pl.when(last)
    def _():
        @pl.loop(0, groups)
        def _(g):
            base, added, both = mixed_projection(g)
            for j in ORDER:
                q_copy(g, j).start()
            pieces = completed(g, low_rank(both, u_prev))
            back_copy(g).start()
            for c in range(chunks):
                w_buf[g, c] = pieces[c]
            for i, piece in enumerate(mixed_four(base, added)):
                p_send[g, 2 + i] = piece

    @pl.when(first)
    def _():
        arrived(loads[2:3])

    @pl.when(own)
    def _():
        arrived(loads[3:])

    def stacked(array):
        return array.astype(wide).reshape(groups * rows, array.shape[-1]).astype(bf16)

    @pl.when(own)
    def _():
        for i in range(nleaf):
            piece = jnp.concatenate(
                [stacked(w_buf[:, c]) for c in range(i * per_leaf, (i + 1) * per_leaf)], axis=1
            )
            four = stacked(p_send[:, 2 + i])
            for c in range(i * per_leaf, (i + 1) * per_leaf):
                l_wide[:, c] = block_part(piece, four, c).reshape(groups, rows, part_width)

        @pl.loop(0, groups)
        def _(g):
            for j in range(1, PEERS):
                q_copy(g, j).wait_recv()
            parts = low_rank(shared(lambda j: p_self[g, j].astype(wide)), u)
            for c, span in enumerate(spans):
                front = (l_wide[g, c] + parts[c]).astype(bf16)
                out[g, :, span] = front
                l_send[g, c] = front

                @pl.when(whole_send)
                def _(c=c):
                    l_copy(g, c).start()

        @pl.loop(0, groups)
        def _(g):
            for j in range(1, PEERS):
                q_copy(g, j).wait_send()

            @pl.when(whole_send)
            def _():
                for c in range(chunks):
                    l_copy(g, c).wait_send()

    @pl.when(split_send)
    def _():
        u_copy().wait_send()

        @pl.loop(0, groups)
        def _(g):
            for c in range(chunks):
                l_copy(g, c).wait_send()
            for j in range(1, PEERS):
                p_copy(g, j).wait_send()
            back_copy(g).wait_recv()
            for c, span in enumerate(spans):
                out[g, :, span] = back_in[g, c]

    @pl.when(split_recv)
    def _():
        @pl.loop(0, groups)
        def _(g):
            back_copy(g).wait_send()


def solution(mesh, groups=GROUPS, whole=WHOLE_SLABS):
    slabs = mesh.shape["slab"]

    def local(sources, leaves, v_rows, u_rows):
        shots, width = sources.shape[1:]
        nleaf, size = leaves.shape[1:3]
        levels, rank = v_rows.shape[1:3]
        rows = shots // groups
        bf16, wide = jnp.bfloat16, jnp.float32
        dma = pltpu.SemaphoreType.DMA
        vmem = pl.BlockSpec(memory_space=pltpu.VMEM)

        def split(dtype):
            return pltpu.VMEM((groups, CHUNKS * nleaf, rows, size // CHUNKS), dtype)

        swept = pl.pallas_call(
            functools.partial(kernel, slabs, whole),
            out_shape=pltpu.VMEM((groups, rows, width), bf16),
            in_specs=[pl.BlockSpec(memory_space=pl.ANY)] * 4,
            out_specs=vmem,
            scratch_shapes=[
                pltpu.VMEM((groups, rows, width), bf16),
                pltpu.VMEM((nleaf, size // 128, size, 128), bf16),
                pltpu.VMEM((width // 128, levels * rank, 128), bf16),
                pltpu.VMEM((width // 128, levels * rank, 128), bf16),
                dma, dma((nleaf, size // 128)), dma((width // 128,)), dma((width // 128,)),
                pltpu.VMEM((width // 128, (levels - 1) * rank, 128), bf16),
                pltpu.VMEM((4, (levels - 1) * rank, 128), bf16),
                split(bf16),
                split(bf16),
                pltpu.VMEM((groups, PEERS, rows, 128), bf16),
                pltpu.VMEM((groups, PEERS, rows, 128), bf16),
                split(bf16),
                split(wide),
                pltpu.VMEM((groups, 2 + nleaf, rows, 128), bf16),
                split(bf16),
                split(bf16),
                dma, dma,
                dma((groups, CHUNKS * nleaf)), dma((groups, CHUNKS * nleaf)),
                dma((groups, PEERS)), dma((groups, PEERS)),
                dma((groups, PEERS)), dma((groups, PEERS)),
                dma((groups,)), dma((groups,)),
            ],
            compiler_params=pltpu.CompilerParams(collective_id=0, has_side_effects=True),
            name="sweep",
        )(
            sources[0].reshape(groups, rows, width),
            leaves[0],
            v_rows[0].reshape(levels * rank, width),
            u_rows[0].reshape(levels * rank, width),
        )
        return swept.reshape(1, shots, width)

    return jax.shard_map(
        local,
        mesh=mesh,
        in_specs=(
            P("slab", None, "hodlr"),
            P("slab", "hodlr", None, None),
            P("slab", None, None, "hodlr"),
            P("slab", None, None, "hodlr"),
        ),
        out_specs=P("slab", None, "hodlr"),
        check_vma=False,
    )
```

```python
import functools

import jax
import jax.numpy as jnp
from jax import lax
from jax.experimental import pallas as pl
from jax.experimental.pallas import tpu as pltpu
from jax.sharding import PartitionSpec as P

MESH = pl.DeviceIdType.MESH
GROUPS = 4
WHOLE_SLABS = 3
PEERS = 8
CHUNKS = 1
ORDER = (4, 6, 5, 7, 2, 3, 1)


def flipped(member, j):
    bits = (lax.rem(member, 2), lax.rem(lax.div(member, 2), 2), lax.div(member, 4))
    total = 0
    for i, bit in enumerate(bits):
        total = total + (1 << i) * ((1 - bit) if (j >> i) & 1 else bit)
    return total


def kernel(
    slabs, whole, src_hbm, leaf_hbm, v_hbm, u_hbm, out,
    src, leaf, v, u, src_sem, leaf_sem, v_sem, u_sem, u_prev, mixed, w_buf, l_in, p_in, p_self, l_send, l_wide, p_send, back, back_in,
    u_ss, u_rs, l_ss, l_rs, p_ss, p_rs, q_ss, q_rs, b_ss, b_rs,
):
    k = lax.axis_index("slab")
    m = lax.axis_index("hodlr")
    groups, rows, width = src.shape
    nleaf, strips, size, _ = leaf.shape
    cross = u_prev.shape[1]
    bf16, wide = jnp.bfloat16, jnp.float32

    first, last = k == 0, k == slabs - 1
    whole_send = k + 1 < whole
    split_send = jnp.logical_and(k + 1 >= whole, k < slabs - 1)
    whole_recv = jnp.logical_and(k >= 1, k < whole)
    split_recv = k >= whole
    own = jnp.logical_or(whole_send, last)
    near_send = jnp.logical_or(k == whole - 1, k == whole)
    near_recv = jnp.logical_or(k == whole, k == whole + 1)
    far_send = jnp.logical_and(k > whole, k < slabs - 1)
    far_recv = k > whole + 1
    chunks, part_width = l_in.shape[1], l_in.shape[3]
    per_leaf, lanes = chunks // nleaf, part_width // 128
    spans = [slice(c * part_width, (c + 1) * part_width) for c in range(chunks)]

    def remote(source, target, send, recv, slab, member):
        return pltpu.make_async_remote_copy(
            src_ref=source, dst_ref=target, send_sem=send, recv_sem=recv,
            device_id=(slab, member), device_id_type=MESH,
        )

    def u_copy(height):
        return remote(u.at[:, pl.ds(0, height)], u_prev.at[:, pl.ds(0, height)], u_ss, u_rs, k + 1, m)

    def l_copy(g, i):
        return remote(l_send.at[g, i], l_in.at[g, i], l_ss.at[g, i], l_rs.at[g, i], k + 1, m)

    def back_copy(g):
        return remote(back.at[g], back_in.at[g], b_ss.at[g], b_rs.at[g], k - 1, m)

    def tile_of(j):
        return 1 if j == 1 else 0

    def p_copy(g, j):
        return remote(
            p_send.at[g, tile_of(j)], p_in.at[g, j], p_ss.at[g, j], p_rs.at[g, j], k + 1, flipped(m, j)
        )

    def q_copy(g, j):
        return remote(
            p_send.at[g, tile_of(j)], p_self.at[g, j], q_ss.at[g, j], q_rs.at[g, j], k, flipped(m, j)
        )

    def strip(source, target, t, sem):
        return pltpu.make_async_copy(source.at[:, pl.ds(t * 128, 128)], target.at[t], sem)

    loads = [
        [pltpu.make_async_copy(src_hbm, src, src_sem)],
        [strip(v_hbm, v, t, v_sem.at[t]) for t in range(nleaf * strips)],
        [strip(leaf_hbm.at[i], leaf.at[i], t, leaf_sem.at[i, t]) for i in range(nleaf) for t in range(strips)],
        [strip(u_hbm, u, t, u_sem.at[t]) for t in range(nleaf * strips)],
    ]

    def arrived(parts):
        for part in parts:
            for load in part:
                load.wait()

    def begin(parts):
        for part in parts:
            for load in part:
                load.start()

    begin(loads[:2])

    @pl.when(jnp.logical_not(first))
    def _():
        begin((loads[3], loads[2]))

    def joined(ref, c, *rows_of):
        return jnp.concatenate([ref[(c * lanes + t, *rows_of)] for t in range(lanes)], axis=1)

    def side(pieces, i):
        return jnp.concatenate(pieces[i * per_leaf : (i + 1) * per_leaf], axis=1)

    barrier = pltpu.get_barrier_semaphore()

    def greet(slab, member):
        pl.semaphore_signal(barrier, inc=1, device_id=(slab, member), device_id_type=MESH)

    @pl.when(own)
    def _():
        for j in range(1, PEERS):
            greet(k, flipped(m, j))

    @pl.when(near_send)
    def _():
        greet(k, flipped(m, 1))

    @pl.when(whole_recv)
    def _():
        greet(k - 1, m)

    @pl.when(whole_send)
    def _():
        greet(k + 1, m)

    @pl.when(split_recv)
    def _():
        for j in range(PEERS):
            greet(k - 1, flipped(m, j))

    @pl.when(split_send)
    def _():
        for j in range(PEERS):
            greet(k + 1, flipped(m, j))

    low = lax.broadcasted_iota(jnp.int32, (rows, 128), 1) < 64

    def upper(read):
        return jnp.where(low, read(4) + read(5) + read(6) + read(7), read(2) + read(3))

    def shared(read):
        return jnp.concatenate([upper(read), read(1)], axis=1).astype(bf16)[:, :cross]

    def low_rank(both, factors):
        return [
            jnp.dot(both, joined(factors, c, slice(0, both.shape[1])), preferred_element_type=wide) for c in range(chunks)
        ]


    def added_to_source(g, c, front):
        return (src[g, :, spans[c]].astype(wide) + front.astype(wide)).astype(bf16)

    def whole_in(g):
        pieces = []
        for c in range(chunks):
            l_copy(g, c).wait_recv()
            pieces.append(added_to_source(g, c, l_in[g, c]))
        return pieces

    def completed(g, parts):
        pieces = []
        for c in range(chunks):
            front = (l_in[g, c].astype(wide) + parts[c]).astype(bf16)
            back[g, c] = front
            pieces.append(added_to_source(g, c, front))
        return pieces

    def near_in(g):
        for j in range(2, PEERS):
            p_copy(g, j).wait_recv()
        for c in range(chunks):
            l_copy(g, c).wait_recv()
        return completed(g, low_rank(upper(lambda j: p_in[g, j].astype(wide)).astype(bf16), u_prev))

    def one_inner(piece, c):
        return lax.dot_general(piece, joined(v, c), (((1,), (1,)), ((), ())), preferred_element_type=wide)

    def inner_of(pieces):
        inner = []
        for i in range(nleaf):
            terms = [one_inner(pieces[c], c) for c in range(i * per_leaf, (i + 1) * per_leaf)]
            inner.append(functools.reduce(jnp.add, terms))
        return inner

    def project(g, pieces):
        inner = inner_of(pieces)
        total = inner[0] + inner[1]
        p_send[g, 0] = total[:, :128].astype(bf16)
        p_send[g, 1] = total[:, 128:].astype(bf16)
        return [jnp.where(low, 0.0, inner[1 - i][:, 128:]).astype(bf16) for i in range(nleaf)]

    def leaf_part(piece, c):
        i, first_strip = c // per_leaf, (c % per_leaf) * lanes
        factor = jnp.concatenate([leaf[i, first_strip + t] for t in range(lanes)], axis=1)
        return jnp.dot(piece, factor, preferred_element_type=wide)

    def four_part(four, c):
        return jnp.dot(four, joined(u, c, slice(cross - 64, None)), preferred_element_type=wide)

    def block_part(piece, four, c):
        return leaf_part(piece, c) + four_part(four, c)

    def send_parts(g, pieces, four):
        for i in range(nleaf):
            piece = side(pieces, i)
            for c in range(i * per_leaf, (i + 1) * per_leaf):
                l_send[g, c] = block_part(piece, four[i], c).astype(bf16)
                l_copy(g, c).start()

    def split_out(g, pieces):
        four = project(g, pieces)
        for j in ORDER:
            p_copy(g, j).start()
        send_parts(g, pieces, four)

    @pl.when(first)
    def _():
        arrived(loads[:2])
        begin(loads[2:])

    met = (
        jnp.where(own, PEERS - 1, 0) + jnp.where(near_send, 1, 0)
        + jnp.where(whole_recv, 1, 0) + jnp.where(whole_send, 1, 0)
        + jnp.where(split_recv, PEERS, 0) + jnp.where(split_send, PEERS, 0)
    )
    pl.semaphore_wait(barrier, met)

    @pl.when(split_send)
    def _():
        arrived(loads[3:])

    @pl.when(near_send)
    def _():
        u_copy(128).start()

    @pl.when(far_send)
    def _():
        u_copy(cross).start()

    @pl.when(jnp.logical_not(first))
    def _():
        arrived(loads[:3])

    @pl.when(near_recv)
    def _():
        u_copy(128).wait_recv()

    @pl.when(far_recv)
    def _():
        u_copy(cross).wait_recv()

    def near_out(g, pieces):
        four = project(g, pieces)
        for j in ORDER[:-1]:
            p_copy(g, j).start()
        q_copy(g, 1).start()
        for i in range(nleaf):
            p_send[g, 2 + i] = four[i]
        for c in range(chunks):
            l_wide[g, c] = leaf_part(side(pieces, c // per_leaf), c)
        q_copy(g, 1).wait_recv()
        for c in range(chunks):
            tile = jnp.where(low, p_self[g, 1].astype(wide), p_send[g, 2 + c // per_leaf].astype(wide)).astype(bf16)
            l_send[g, c] = (l_wide[g, c] + four_part(tile, c)).astype(bf16)
            l_copy(g, c).start()

    @pl.when(jnp.logical_and(whole_recv, near_send))
    def _():
        @pl.loop(0, groups)
        def _(g):
            near_out(g, whole_in(g))

    @pl.when(k == whole)
    def _():
        @pl.loop(0, groups)
        def _(g):
            near_out(g, near_in(g))
            back_copy(g).start()

    @pl.when(k == whole + 1)
    def _():
        @pl.loop(0, groups)
        def _(g):
            split_out(g, near_in(g))
            back_copy(g).start()

    def mixed_projection(g):
        terms = []
        for c in range(chunks):
            l_copy(g, c).wait_recv()
            terms.append(one_inner(added_to_source(g, c, l_in[g, c]), c))
        base = [functools.reduce(jnp.add, terms[i * per_leaf : (i + 1) * per_leaf]) for i in range(nleaf)]
        ready = base[0] + base[1]
        for j in range(1, PEERS):
            p_copy(g, j).wait_recv()
        both = shared(lambda j: p_in[g, j].astype(wide))
        added = jnp.dot(both, jnp.concatenate([mixed[t] for t in range(4)], axis=1), preferred_element_type=wide)
        p_send[g, 0] = (ready[:, :128] + added[:, :128]).astype(bf16)
        p_send[g, 1] = (ready[:, 128:] + added[:, 128:256]).astype(bf16)
        return base, added, both

    def mixed_four(base, added):
        four = []
        for i in range(nleaf):
            value = base[1 - i][:, 128:] + added[:, 256 + 128 * i : 384 + 128 * i]
            four.append(jnp.where(low, 0.0, value).astype(bf16))
        return four

    @pl.when(far_recv)
    def _():
        inner = inner_of([joined(u_prev, c) for c in range(chunks)])
        total = (inner[0] + inner[1]).astype(bf16)
        mixed[0] = total[:, :128]
        mixed[1] = total[:, 128:]
        mixed[2] = inner[1][:, 128:].astype(bf16)
        mixed[3] = inner[0][:, 128:].astype(bf16)

    @pl.when(jnp.logical_and(far_recv, split_send))
    def _():
        @pl.loop(0, groups)
        def _(g):
            base, added, both = mixed_projection(g)
            for j in ORDER:
                p_copy(g, j).start()
            pieces = completed(g, low_rank(both, u_prev))
            send_parts(g, pieces, mixed_four(base, added))
            back_copy(g).start()

    @pl.when(first)
    def _():
        @pl.loop(0, groups)
        def _(g):
            pieces = [src[g, :, span] for span in spans]
            for i, piece in enumerate(project(g, pieces)):
                p_send[g, 2 + i] = piece
            for j in ORDER:
                q_copy(g, j).start()
            for c in range(chunks):
                w_buf[g, c] = pieces[c]

    @pl.when(jnp.logical_and(whole_recv, whole_send))
    def _():
        @pl.loop(0, groups)
        def _(g):
            pieces = whole_in(g)
            for i, piece in enumerate(project(g, pieces)):
                p_send[g, 2 + i] = piece
            for j in ORDER:
                q_copy(g, j).start()
            for c in range(chunks):
                w_buf[g, c] = pieces[c]

    @pl.when(last)
    def _():
        @pl.loop(0, groups)
        def _(g):
            base, added, both = mixed_projection(g)
            for j in ORDER:
                q_copy(g, j).start()
            pieces = completed(g, low_rank(both, u_prev))
            back_copy(g).start()
            for c in range(chunks):
                w_buf[g, c] = pieces[c]
            for i, piece in enumerate(mixed_four(base, added)):
                p_send[g, 2 + i] = piece

    @pl.when(first)
    def _():
        arrived(loads[2:3])

    @pl.when(own)
    def _():
        arrived(loads[3:])

    def stacked(array):
        return array.astype(wide).reshape(groups * rows, array.shape[-1]).astype(bf16)

    @pl.when(own)
    def _():
        for i in range(nleaf):
            piece = jnp.concatenate(
                [stacked(w_buf[:, c]) for c in range(i * per_leaf, (i + 1) * per_leaf)], axis=1
            )
            four = stacked(p_send[:, 2 + i])
            for c in range(i * per_leaf, (i + 1) * per_leaf):
                l_wide[:, c] = block_part(piece, four, c).reshape(groups, rows, part_width)

        @pl.loop(0, groups)
        def _(g):
            for j in range(1, PEERS):
                q_copy(g, j).wait_recv()
            parts = low_rank(shared(lambda j: p_self[g, j].astype(wide)), u)
            for c, span in enumerate(spans):
                front = (l_wide[g, c] + parts[c]).astype(bf16)
                out[g, :, span] = front
                l_send[g, c] = front

                @pl.when(whole_send)
                def _(c=c):
                    l_copy(g, c).start()

        @pl.loop(0, groups)
        def _(g):
            for j in range(1, PEERS):
                q_copy(g, j).wait_send()

            @pl.when(whole_send)
            def _():
                for c in range(chunks):
                    l_copy(g, c).wait_send()

    @pl.when(split_send)
    def _():
        @pl.when(near_send)
        def _():
            u_copy(128).wait_send()

            @pl.loop(0, groups)
            def _(g):
                q_copy(g, 1).wait_send()

        @pl.when(far_send)
        def _():
            u_copy(cross).wait_send()

            @pl.loop(0, groups)
            def _(g):
                p_copy(g, 1).wait_send()

        @pl.loop(0, groups)
        def _(g):
            for c in range(chunks):
                l_copy(g, c).wait_send()
            for j in range(2, PEERS):
                p_copy(g, j).wait_send()
            back_copy(g).wait_recv()
            for c, span in enumerate(spans):
                out[g, :, span] = back_in[g, c]

    @pl.when(split_recv)
    def _():
        @pl.loop(0, groups)
        def _(g):
            back_copy(g).wait_send()


def solution(mesh, groups=GROUPS, whole=WHOLE_SLABS):
    slabs = mesh.shape["slab"]

    def local(sources, leaves, v_rows, u_rows):
        shots, width = sources.shape[1:]
        nleaf, size = leaves.shape[1:3]
        levels, rank = v_rows.shape[1:3]
        rows = shots // groups
        bf16, wide = jnp.bfloat16, jnp.float32
        dma = pltpu.SemaphoreType.DMA
        vmem = pl.BlockSpec(memory_space=pltpu.VMEM)

        def split(dtype):
            return pltpu.VMEM((groups, CHUNKS * nleaf, rows, size // CHUNKS), dtype)

        swept = pl.pallas_call(
            functools.partial(kernel, slabs, whole),
            out_shape=pltpu.VMEM((groups, rows, width), bf16),
            in_specs=[pl.BlockSpec(memory_space=pl.ANY)] * 4,
            out_specs=vmem,
            scratch_shapes=[
                pltpu.VMEM((groups, rows, width), bf16),
                pltpu.VMEM((nleaf, size // 128, size, 128), bf16),
                pltpu.VMEM((width // 128, levels * rank, 128), bf16),
                pltpu.VMEM((width // 128, levels * rank, 128), bf16),
                dma, dma((nleaf, size // 128)), dma((width // 128,)), dma((width // 128,)),
                pltpu.VMEM((width // 128, (levels - 1) * rank, 128), bf16),
                pltpu.VMEM((4, (levels - 1) * rank, 128), bf16),
                split(bf16),
                split(bf16),
                pltpu.VMEM((groups, PEERS, rows, 128), bf16),
                pltpu.VMEM((groups, PEERS, rows, 128), bf16),
                split(bf16),
                split(wide),
                pltpu.VMEM((groups, 2 + nleaf, rows, 128), bf16),
                split(bf16),
                split(bf16),
                dma, dma,
                dma((groups, CHUNKS * nleaf)), dma((groups, CHUNKS * nleaf)),
                dma((groups, PEERS)), dma((groups, PEERS)),
                dma((groups, PEERS)), dma((groups, PEERS)),
                dma((groups,)), dma((groups,)),
            ],
            compiler_params=pltpu.CompilerParams(collective_id=0, has_side_effects=True),
            name="sweep",
        )(
            sources[0].reshape(groups, rows, width),
            leaves[0],
            v_rows[0].reshape(levels * rank, width),
            u_rows[0].reshape(levels * rank, width),
        )
        return swept.reshape(1, shots, width)

    return jax.shard_map(
        local,
        mesh=mesh,
        in_specs=(
            P("slab", None, "hodlr"),
            P("slab", "hodlr", None, None),
            P("slab", None, None, "hodlr"),
            P("slab", None, None, "hodlr"),
        ),
        out_specs=P("slab", None, "hodlr"),
        check_vma=False,
    )
```

```python
import functools

import jax
import jax.numpy as jnp
from jax import lax
from jax.experimental import pallas as pl
from jax.experimental.pallas import tpu as pltpu
from jax.sharding import PartitionSpec as P

MESH = pl.DeviceIdType.MESH
GROUPS = 4
WHOLE_SLABS = 3
PEERS = 8
CHUNKS = 1
ORDER = (4, 6, 5, 7, 2, 3, 1)


def flipped(member, j):
    bits = (lax.rem(member, 2), lax.rem(lax.div(member, 2), 2), lax.div(member, 4))
    total = 0
    for i, bit in enumerate(bits):
        total = total + (1 << i) * ((1 - bit) if (j >> i) & 1 else bit)
    return total


def kernel(
    slabs, whole, src_hbm, leaf_hbm, v_hbm, u_hbm, out,
    src, leaf, v, u, src_sem, leaf_sem, v_sem, u_sem, u_prev, mixed, w_buf, l_in, p_in, p_self, l_send, l_wide, p_send, back, back_in,
    u_ss, u_rs, l_ss, l_rs, p_ss, p_rs, q_ss, q_rs, b_ss, b_rs,
):
    k = lax.axis_index("slab")
    m = lax.axis_index("hodlr")
    groups, rows, width = src.shape
    nleaf, strips, size, _ = leaf.shape
    cross = u_prev.shape[1]
    bf16, wide = jnp.bfloat16, jnp.float32

    first, last = k == 0, k == slabs - 1
    whole_send = k + 1 < whole
    split_send = jnp.logical_and(k + 1 >= whole, k < slabs - 1)
    whole_recv = jnp.logical_and(k >= 1, k < whole)
    split_recv = k >= whole
    own = jnp.logical_or(whole_send, last)
    near_send = jnp.logical_or(k == whole - 1, k == whole)
    near_recv = jnp.logical_or(k == whole, k == whole + 1)
    far_send = jnp.logical_and(k > whole, k < slabs - 1)
    far_recv = k > whole + 1
    chunks, part_width = l_in.shape[1], l_in.shape[3]
    per_leaf, lanes = chunks // nleaf, part_width // 128
    spans = [slice(c * part_width, (c + 1) * part_width) for c in range(chunks)]

    def remote(source, target, send, recv, slab, member):
        return pltpu.make_async_remote_copy(
            src_ref=source, dst_ref=target, send_sem=send, recv_sem=recv,
            device_id=(slab, member), device_id_type=MESH,
        )

    def u_copy(height):
        return remote(u.at[:, pl.ds(0, height)], u_prev.at[:, pl.ds(0, height)], u_ss, u_rs, k + 1, m)

    def l_copy(g, i):
        return remote(l_send.at[g, i], l_in.at[g, i], l_ss.at[g, i], l_rs.at[g, i], k + 1, m)

    def back_copy(g):
        return remote(back.at[g], back_in.at[g], b_ss.at[g], b_rs.at[g], k - 1, m)

    def tile_of(j):
        return 1 if j == 1 else 0

    def p_copy(g, j):
        return remote(
            p_send.at[g, tile_of(j)], p_in.at[g, j], p_ss.at[g, j], p_rs.at[g, j], k + 1, flipped(m, j)
        )

    def q_copy(g, j):
        return remote(
            p_send.at[g, tile_of(j)], p_self.at[g, j], q_ss.at[g, j], q_rs.at[g, j], k, flipped(m, j)
        )

    def strip(source, target, t, sem):
        return pltpu.make_async_copy(source.at[:, pl.ds(t * 128, 128)], target.at[t], sem)

    loads = [
        [pltpu.make_async_copy(src_hbm, src, src_sem)],
        [strip(v_hbm, v, t, v_sem.at[t]) for t in range(nleaf * strips)],
        [strip(leaf_hbm.at[i], leaf.at[i], t, leaf_sem.at[i, t]) for i in range(nleaf) for t in range(strips)],
        [strip(u_hbm, u, t, u_sem.at[t]) for t in range(nleaf * strips)],
    ]

    def arrived(parts):
        for part in parts:
            for load in part:
                load.wait()

    def begin(parts):
        for part in parts:
            for load in part:
                load.start()

    def joined(ref, c, *rows_of):
        return jnp.concatenate([ref[(c * lanes + t, *rows_of)] for t in range(lanes)], axis=1)

    def side(pieces, i):
        return jnp.concatenate(pieces[i * per_leaf : (i + 1) * per_leaf], axis=1)

    barrier = pltpu.get_barrier_semaphore()

    def greet(slab, member):
        pl.semaphore_signal(barrier, inc=1, device_id=(slab, member), device_id_type=MESH)

    @pl.when(own)
    def _():
        for j in ORDER:
            greet(k, flipped(m, j))

    @pl.when(near_send)
    def _():
        greet(k, flipped(m, 1))

    @pl.when(whole_recv)
    def _():
        greet(k - 1, m)

    @pl.when(whole_send)
    def _():
        greet(k + 1, m)

    @pl.when(split_recv)
    def _():
        for j in range(PEERS):
            greet(k - 1, flipped(m, j))

    @pl.when(split_send)
    def _():
        for j in range(PEERS):
            greet(k + 1, flipped(m, j))

    begin(loads[:2])

    @pl.when(jnp.logical_not(first))
    def _():
        begin((loads[3], loads[2]))

    low = lax.broadcasted_iota(jnp.int32, (rows, 128), 1) < 64

    def upper(read):
        return jnp.where(low, read(4) + read(5) + read(6) + read(7), read(2) + read(3))

    def shared(read):
        return jnp.concatenate([upper(read), read(1)], axis=1).astype(bf16)[:, :cross]

    def low_rank(both, factors):
        return [
            jnp.dot(both, joined(factors, c, slice(0, both.shape[1])), preferred_element_type=wide) for c in range(chunks)
        ]


    def added_to_source(g, c, front):
        return (src[g, :, spans[c]].astype(wide) + front.astype(wide)).astype(bf16)

    def whole_in(g):
        pieces = []
        for c in range(chunks):
            l_copy(g, c).wait_recv()
            pieces.append(added_to_source(g, c, l_in[g, c]))
        return pieces

    def completed(g, parts):
        pieces = []
        for c in range(chunks):
            front = (l_in[g, c].astype(wide) + parts[c]).astype(bf16)
            back[g, c] = front
            pieces.append(added_to_source(g, c, front))
        return pieces

    def near_in(g):
        for j in range(2, PEERS):
            p_copy(g, j).wait_recv()
        for c in range(chunks):
            l_copy(g, c).wait_recv()
        return completed(g, low_rank(upper(lambda j: p_in[g, j].astype(wide)).astype(bf16), u_prev))

    def one_inner(piece, c):
        return lax.dot_general(piece, joined(v, c), (((1,), (1,)), ((), ())), preferred_element_type=wide)

    def inner_of(pieces):
        inner = []
        for i in range(nleaf):
            terms = [one_inner(pieces[c], c) for c in range(i * per_leaf, (i + 1) * per_leaf)]
            inner.append(functools.reduce(jnp.add, terms))
        return inner

    def project(g, pieces):
        inner = inner_of(pieces)
        total = inner[0] + inner[1]
        p_send[g, 0] = total[:, :128].astype(bf16)
        p_send[g, 1] = total[:, 128:].astype(bf16)
        return [jnp.where(low, 0.0, inner[1 - i][:, 128:]).astype(bf16) for i in range(nleaf)]

    def leaf_part(piece, c):
        i, first_strip = c // per_leaf, (c % per_leaf) * lanes
        factor = jnp.concatenate([leaf[i, first_strip + t] for t in range(lanes)], axis=1)
        return jnp.dot(piece, factor, preferred_element_type=wide)

    def four_part(four, c):
        return jnp.dot(four, joined(u, c, slice(cross - 64, None)), preferred_element_type=wide)

    def block_part(piece, four, c):
        return leaf_part(piece, c) + four_part(four, c)

    def send_parts(g, pieces, four):
        for i in range(nleaf):
            piece = side(pieces, i)
            for c in range(i * per_leaf, (i + 1) * per_leaf):
                l_send[g, c] = block_part(piece, four[i], c).astype(bf16)
                l_copy(g, c).start()

    def split_out(g, pieces):
        four = project(g, pieces)
        for j in ORDER:
            p_copy(g, j).start()
        send_parts(g, pieces, four)

    @pl.when(first)
    def _():
        arrived(loads[:2])
        begin(loads[2:])

    met = (
        jnp.where(own, PEERS - 1, 0) + jnp.where(near_send, 1, 0)
        + jnp.where(whole_recv, 1, 0) + jnp.where(whole_send, 1, 0)
        + jnp.where(split_recv, PEERS, 0) + jnp.where(split_send, PEERS, 0)
    )
    pl.semaphore_wait(barrier, met)

    @pl.when(split_send)
    def _():
        arrived(loads[3:])

    @pl.when(near_send)
    def _():
        u_copy(128).start()

    @pl.when(far_send)
    def _():
        u_copy(cross).start()

    @pl.when(jnp.logical_not(first))
    def _():
        arrived(loads[:3])

    @pl.when(near_recv)
    def _():
        u_copy(128).wait_recv()

    @pl.when(far_recv)
    def _():
        u_copy(cross).wait_recv()

    def near_out(g, pieces):
        four = project(g, pieces)
        for j in ORDER[:-1]:
            p_copy(g, j).start()
        q_copy(g, 1).start()
        for i in range(nleaf):
            p_send[g, 2 + i] = four[i]
        for c in range(chunks):
            l_wide[g, c] = leaf_part(side(pieces, c // per_leaf), c)
        q_copy(g, 1).wait_recv()
        for c in range(chunks):
            tile = jnp.where(low, p_self[g, 1].astype(wide), p_send[g, 2 + c // per_leaf].astype(wide)).astype(bf16)
            l_send[g, c] = (l_wide[g, c] + four_part(tile, c)).astype(bf16)
            l_copy(g, c).start()

    @pl.when(jnp.logical_and(whole_recv, near_send))
    def _():
        @pl.loop(0, groups)
        def _(g):
            near_out(g, whole_in(g))

    @pl.when(k == whole)
    def _():
        @pl.loop(0, groups)
        def _(g):
            near_out(g, near_in(g))
            back_copy(g).start()

    @pl.when(k == whole + 1)
    def _():
        @pl.loop(0, groups)
        def _(g):
            split_out(g, near_in(g))
            back_copy(g).start()

    def mixed_projection(g):
        terms = []
        for c in range(chunks):
            l_copy(g, c).wait_recv()
            terms.append(one_inner(added_to_source(g, c, l_in[g, c]), c))
        base = [functools.reduce(jnp.add, terms[i * per_leaf : (i + 1) * per_leaf]) for i in range(nleaf)]
        ready = base[0] + base[1]
        for j in range(1, PEERS):
            p_copy(g, j).wait_recv()
        both = shared(lambda j: p_in[g, j].astype(wide))
        added = jnp.dot(both, jnp.concatenate([mixed[t] for t in range(4)], axis=1), preferred_element_type=wide)
        p_send[g, 0] = (ready[:, :128] + added[:, :128]).astype(bf16)
        p_send[g, 1] = (ready[:, 128:] + added[:, 128:256]).astype(bf16)
        return base, added, both

    def mixed_four(base, added):
        four = []
        for i in range(nleaf):
            value = base[1 - i][:, 128:] + added[:, 256 + 128 * i : 384 + 128 * i]
            four.append(jnp.where(low, 0.0, value).astype(bf16))
        return four

    @pl.when(far_recv)
    def _():
        inner = inner_of([joined(u_prev, c) for c in range(chunks)])
        total = (inner[0] + inner[1]).astype(bf16)
        mixed[0] = total[:, :128]
        mixed[1] = total[:, 128:]
        mixed[2] = inner[1][:, 128:].astype(bf16)
        mixed[3] = inner[0][:, 128:].astype(bf16)

    @pl.when(jnp.logical_and(far_recv, split_send))
    def _():
        @pl.loop(0, groups)
        def _(g):
            base, added, both = mixed_projection(g)
            for j in ORDER:
                p_copy(g, j).start()
            pieces = completed(g, low_rank(both, u_prev))
            send_parts(g, pieces, mixed_four(base, added))
            back_copy(g).start()

    @pl.when(first)
    def _():
        @pl.loop(0, groups)
        def _(g):
            pieces = [src[g, :, span] for span in spans]
            for i, piece in enumerate(project(g, pieces)):
                p_send[g, 2 + i] = piece
            for j in ORDER:
                q_copy(g, j).start()
            for c in range(chunks):
                w_buf[g, c] = pieces[c]

    @pl.when(jnp.logical_and(whole_recv, whole_send))
    def _():
        @pl.loop(0, groups)
        def _(g):
            pieces = whole_in(g)
            for i, piece in enumerate(project(g, pieces)):
                p_send[g, 2 + i] = piece
            for j in ORDER:
                q_copy(g, j).start()
            for c in range(chunks):
                w_buf[g, c] = pieces[c]

    @pl.when(last)
    def _():
        @pl.loop(0, groups)
        def _(g):
            base, added, both = mixed_projection(g)
            for j in ORDER:
                q_copy(g, j).start()
            pieces = completed(g, low_rank(both, u_prev))
            back_copy(g).start()
            for c in range(chunks):
                w_buf[g, c] = pieces[c]
            for i, piece in enumerate(mixed_four(base, added)):
                p_send[g, 2 + i] = piece

    @pl.when(first)
    def _():
        arrived(loads[2:3])

    @pl.when(own)
    def _():
        arrived(loads[3:])

    def stacked(array):
        return array.astype(wide).reshape(groups * rows, array.shape[-1]).astype(bf16)

    @pl.when(own)
    def _():
        for i in range(nleaf):
            piece = jnp.concatenate(
                [stacked(w_buf[:, c]) for c in range(i * per_leaf, (i + 1) * per_leaf)], axis=1
            )
            four = stacked(p_send[:, 2 + i])
            for c in range(i * per_leaf, (i + 1) * per_leaf):
                l_wide[:, c] = block_part(piece, four, c).reshape(groups, rows, part_width)

        @pl.loop(0, groups)
        def _(g):
            for j in range(1, PEERS):
                q_copy(g, j).wait_recv()
            parts = low_rank(shared(lambda j: p_self[g, j].astype(wide)), u)
            for c, span in enumerate(spans):
                front = (l_wide[g, c] + parts[c]).astype(bf16)
                out[g, :, span] = front
                l_send[g, c] = front

                @pl.when(whole_send)
                def _(c=c):
                    l_copy(g, c).start()

        @pl.loop(0, groups)
        def _(g):
            for j in range(1, PEERS):
                q_copy(g, j).wait_send()

            @pl.when(whole_send)
            def _():
                for c in range(chunks):
                    l_copy(g, c).wait_send()

    @pl.when(split_send)
    def _():
        @pl.when(near_send)
        def _():
            u_copy(128).wait_send()

            @pl.loop(0, groups)
            def _(g):
                q_copy(g, 1).wait_send()

        @pl.when(far_send)
        def _():
            u_copy(cross).wait_send()

            @pl.loop(0, groups)
            def _(g):
                p_copy(g, 1).wait_send()

        @pl.loop(0, groups)
        def _(g):
            for c in range(chunks):
                l_copy(g, c).wait_send()
            for j in range(2, PEERS):
                p_copy(g, j).wait_send()
            back_copy(g).wait_recv()
            for c, span in enumerate(spans):
                out[g, :, span] = back_in[g, c]

    @pl.when(split_recv)
    def _():
        @pl.loop(0, groups)
        def _(g):
            back_copy(g).wait_send()


def solution(mesh, groups=GROUPS, whole=WHOLE_SLABS):
    slabs = mesh.shape["slab"]

    def local(sources, leaves, v_rows, u_rows):
        shots, width = sources.shape[1:]
        nleaf, size = leaves.shape[1:3]
        levels, rank = v_rows.shape[1:3]
        rows = shots // groups
        bf16, wide = jnp.bfloat16, jnp.float32
        dma = pltpu.SemaphoreType.DMA
        vmem = pl.BlockSpec(memory_space=pltpu.VMEM)

        def split(dtype):
            return pltpu.VMEM((groups, CHUNKS * nleaf, rows, size // CHUNKS), dtype)

        swept = pl.pallas_call(
            functools.partial(kernel, slabs, whole),
            out_shape=pltpu.VMEM((groups, rows, width), bf16),
            in_specs=[pl.BlockSpec(memory_space=pl.ANY)] * 4,
            out_specs=vmem,
            scratch_shapes=[
                pltpu.VMEM((groups, rows, width), bf16),
                pltpu.VMEM((nleaf, size // 128, size, 128), bf16),
                pltpu.VMEM((width // 128, levels * rank, 128), bf16),
                pltpu.VMEM((width // 128, levels * rank, 128), bf16),
                dma, dma((nleaf, size // 128)), dma((width // 128,)), dma((width // 128,)),
                pltpu.VMEM((width // 128, (levels - 1) * rank, 128), bf16),
                pltpu.VMEM((4, (levels - 1) * rank, 128), bf16),
                split(bf16),
                split(bf16),
                pltpu.VMEM((groups, PEERS, rows, 128), bf16),
                pltpu.VMEM((groups, PEERS, rows, 128), bf16),
                split(bf16),
                split(wide),
                pltpu.VMEM((groups, 2 + nleaf, rows, 128), bf16),
                split(bf16),
                split(bf16),
                dma, dma,
                dma((groups, CHUNKS * nleaf)), dma((groups, CHUNKS * nleaf)),
                dma((groups, PEERS)), dma((groups, PEERS)),
                dma((groups, PEERS)), dma((groups, PEERS)),
                dma((groups,)), dma((groups,)),
            ],
            compiler_params=pltpu.CompilerParams(collective_id=0, has_side_effects=True),
            name="sweep",
        )(
            sources[0].reshape(groups, rows, width),
            leaves[0],
            v_rows[0].reshape(levels * rank, width),
            u_rows[0].reshape(levels * rank, width),
        )
        return swept.reshape(1, shots, width)

    return jax.shard_map(
        local,
        mesh=mesh,
        in_specs=(
            P("slab", None, "hodlr"),
            P("slab", "hodlr", None, None),
            P("slab", None, None, "hodlr"),
            P("slab", None, None, "hodlr"),
        ),
        out_specs=P("slab", None, "hodlr"),
        check_vma=False,
    )
```
